32 devices in a mesh: stream: 16 (over z, y, x), cross: 2 (over core).
Axes of the slice: x: 2, y: 2, z: 4, core: 2. Of those that a mesh axis runs over, the one named last changes fastest.
Arguments:
- vector: float32 [64, 4, 320], P('stream', 'cross'), may hold values from -2.5 to 2.5
- inverses: float32 [64, 4, 320, 320], P('stream', 'cross'), may hold values from -0.04 to 1
- lift_maps: float32 [4, 320, 80], replicated, may hold values from -1 to 1
- jacobians: float32 [64, 4, 4, 5, 5, 16], P('stream', 'cross'), may hold values from -0.2 to 1.43
- orient: int32 [64, 4], P('stream', 'cross'), may hold values from 0 to 7
Outputs:
- solution: float32 [64, 4, 320], P('stream', 'cross')
The draws below stay inside these ranges and needn't reach their ends.
All inputs are finite; a program needn't handle non-finite values.
Results may differ from the reference program's by a relative error of at most 0.0003.
Values sent between devices are 32-bit elements; how exact they have to be, the bound alone decides.
A program may use at most 64 MiB of HBM per device.

```python
import jax
import jax.numpy as jnp
from jax import lax

ORDER = 3
VARS = 5
NODES = 64
FACE = 16
BLOCK = 320
TRACE = 80
PASSES = 2
TOTAL_LAYERS = 64
TOTAL_CELLS = 4


def diagonal_draw(key):
    return jax.random.uniform(jax.random.fold_in(key, 11), (TOTAL_LAYERS, TOTAL_CELLS, BLOCK), jnp.float32, 0.7, 1.0)


def draw_inverses(key, part):
    full_shape = (TOTAL_LAYERS, TOTAL_CELLS, BLOCK, BLOCK)
    diagonal = diagonal_draw(key)
    key_off = jax.random.fold_in(key, 12)
    spread = jnp.clip(0.0095 * jax.random.normal(key_off, full_shape, jnp.float32), -0.04, 0.04)
    eye_mask = (jnp.arange(BLOCK)[:, None] == jnp.arange(BLOCK)[None, :]).astype(jnp.float32)
    return eye_mask * diagonal[..., None] + (1.0 - eye_mask) * spread


def draw_lift_maps(key, part):
    rows = jnp.arange(BLOCK, dtype=jnp.int32)
    var_of = rows // NODES
    remain = rows % NODES
    layer_of = remain // FACE
    node_of = remain % FACE
    trace_of = var_of * FACE + node_of
    columns = jnp.arange(TRACE, dtype=jnp.int32)
    match = (trace_of[:, None] == columns[None, :]).astype(jnp.float32)
    high_face = (layer_of == ORDER)[:, None]
    low_face = (layer_of == 0)[:, None]
    scale = 1.0 / jnp.sqrt(jnp.float32(TRACE))
    noise = jnp.clip(scale * jax.random.normal(key, (4, BLOCK, TRACE), jnp.float32), -4.0 * scale, 4.0 * scale)
    stream_low = jnp.where(high_face, -match, 0.35 * noise[0])
    stream_high = jnp.where(low_face, -match, 0.35 * noise[1])
    return jnp.stack([stream_low, stream_high, noise[2], noise[3]])


def draw_jacobians(key, part):
    extent = ORDER + 1
    full_shape = (TOTAL_LAYERS, TOTAL_CELLS, 4, VARS, VARS, FACE)
    rate_shape = (TOTAL_LAYERS, TOTAL_CELLS, 2, VARS, FACE)
    diagonal = diagonal_draw(key).reshape(TOTAL_LAYERS, TOTAL_CELLS, VARS, extent, FACE)
    face_diagonal = jnp.stack([diagonal[:, :, :, extent - 1], diagonal[:, :, :, 0]], axis=2)
    slow_share = 0.5
    sluggish_part = jax.random.bernoulli(jax.random.fold_in(key, 21), slow_share, (1, TOTAL_CELLS, 2, VARS, FACE))
    spread_power = jax.random.uniform(jax.random.fold_in(key, 22), (1, TOTAL_CELLS, 2, VARS, FACE), jnp.float32, 0.5, 1.5)
    gentle_decay_rate = jnp.exp(jnp.log(jnp.float32(0.25)) / TOTAL_LAYERS * spread_power)
    quick_decay_rate = jax.random.uniform(jax.random.fold_in(key, 23), rate_shape, jnp.float32, 0.85, 0.95)
    spike_factor = jax.random.bernoulli(jax.random.fold_in(key, 24), 2.0 / TOTAL_LAYERS, (TOTAL_LAYERS, TOTAL_CELLS, 2, 1, 1))
    residual_loss = jax.random.uniform(jax.random.fold_in(key, 25), rate_shape, jnp.float32, 0.6, 0.8)
    decay_rate = jnp.where(sluggish_part, gentle_decay_rate * jnp.where(spike_factor, residual_loss, 1.0), quick_decay_rate)
    stream_diagonal = decay_rate / face_diagonal
    cross_diagonal = jax.random.uniform(jax.random.fold_in(key, 26), rate_shape, jnp.float32, 0.5, 1.0)
    diagonal_all = jnp.concatenate([stream_diagonal, cross_diagonal], axis=2)
    face_scale = jnp.array([0.02, 0.02, 0.08, 0.08], jnp.float32)[None, None, :, None, None, None]
    key_off = jax.random.fold_in(key, 27)
    coupling = jnp.clip(face_scale * jax.random.normal(key_off, full_shape, jnp.float32), -2.5 * face_scale, 2.5 * face_scale)
    eye_mask = (jnp.arange(VARS)[:, None] == jnp.arange(VARS)[None, :]).astype(jnp.float32)[:, :, None]
    return eye_mask * diagonal_all[:, :, :, :, None, :] + (1.0 - eye_mask) * coupling


def touch_ends(entries, own_key, smallest, top_value):
    place = [jax.random.randint(jax.random.fold_in(own_key, axis), (), 0, length) for axis, length in enumerate(entries.shape)]
    longest = entries.shape.index(max(entries.shape))
    neighbour = place[:longest] + [(place[longest] + 1) % entries.shape[longest]] + place[longest + 1:]
    return entries.at[tuple(place)].set(smallest).at[tuple(neighbour)].set(top_value)


def shard_levels(own_key, shape, pieces, least, top_value):
    loudness = 1.0
    for position, blocks in pieces:
        steps = jax.random.uniform(jax.random.fold_in(jax.random.fold_in(own_key, 6), position), (blocks,), jnp.float32, least / len(pieces), top_value / len(pieces))
        loudness = loudness * jnp.repeat(jnp.exp(steps), shape[position] // blocks).reshape((-1,) + (1,) * (len(shape) - 1 - position))
    return loudness


def gaussian(own_key, shape, scale, bound, cuts=(), held_as=jnp.bfloat16):
    values = jax.random.normal(own_key, shape, jnp.float32) * scale
    if len(cuts) > 0:
        values = shard_levels(own_key, shape, cuts, -0.22, 0.18) * values
    return jnp.clip(values, min=-bound, max=bound).astype(held_as)


def setup_inputs(seed: int = 0) -> dict:
    arg_keys = jax.random.split(jax.random.key(seed), 6)
    return {
        "vector": gaussian(arg_keys[0], (TOTAL_LAYERS, TOTAL_CELLS, BLOCK), 0.25, 2.5, ((0, 16), (1, 2)), jnp.float32),
        "inverses": draw_inverses(jax.random.fold_in(arg_keys[5], 71), 0),
        "lift_maps": draw_lift_maps(jax.random.fold_in(arg_keys[5], 71), 0),
        "jacobians": draw_jacobians(jax.random.fold_in(arg_keys[5], 71), 0),
        "orient": touch_ends(jax.random.randint(arg_keys[4], (TOTAL_LAYERS, TOTAL_CELLS), 0, 8), jax.random.fold_in(arg_keys[4], 1), 0, 7).astype(jnp.int32),
    }


HIGHEST = lax.Precision.HIGHEST


def face_traces(field_values):
    extent = ORDER + 1
    node_cube = field_values.reshape(field_values.shape[:-1] + (VARS, extent, extent, extent))
    face_shape = field_values.shape[:-1] + (VARS, extent * extent)
    return (node_cube[..., 0, :, :].reshape(face_shape),
            node_cube[..., extent - 1, :, :].reshape(face_shape),
            node_cube[..., :, 0, :].reshape(face_shape),
            node_cube[..., :, extent - 1, :].reshape(face_shape))


def couple(lift_matrix, jacobian_face, face_trace):
    mixed_trace = jnp.einsum('...awf,...wf->...af', jacobian_face, face_trace, precision=HIGHEST)
    flat_trace = mixed_trace.reshape(mixed_trace.shape[:-2] + (TRACE,))
    return jnp.einsum('...t,rt->...r', flat_trace, lift_matrix, precision=HIGHEST)


def orient_tables():
    extent = ORDER + 1
    nodes_index = jnp.arange(extent * extent, dtype=jnp.int32)
    tables = []
    for variant in range(8):
        first_axis = nodes_index // extent
        second_axis = nodes_index % extent
        if variant % 2 == 1:
            first_axis, second_axis = second_axis, first_axis
        if (variant // 2) % 2 == 1:
            first_axis = extent - 1 - first_axis
        if (variant // 4) % 2 == 1:
            second_axis = extent - 1 - second_axis
        source_node = first_axis * extent + second_axis
        tables.append((source_node[:, None] == nodes_index[None, :]).astype(jnp.float32))
    return jnp.stack(tables)


def cross_load(field_values, lift_maps, jacobians, orient):
    chosen = (orient[..., None] == jnp.arange(8, dtype=jnp.int32)).astype(jnp.float32)
    picked = jnp.einsum('lco,odf->lcdf', chosen, orient_tables(), precision=HIGHEST)
    traces = face_traces(field_values)
    low_trace, high_trace = traces[2], traces[3]
    back_trace = jnp.einsum('lcdf,lcvd->lcvf', picked, low_trace, precision=HIGHEST)
    zero_rim = jnp.zeros_like(high_trace[:, :1])
    from_left = jnp.concatenate([zero_rim, high_trace[:, :-1]], axis=1)
    from_right = jnp.concatenate([back_trace[:, 1:], zero_rim], axis=1)
    mapped = jnp.einsum('lcdf,lcvf->lcvd', picked, from_left, precision=HIGHEST)
    return couple(lift_maps[2], jacobians[:, :, 2], mapped) + couple(lift_maps[3], jacobians[:, :, 3], from_right)


def line_sweep(right_side, inverses, lift_maps, jacobians):
    def forward(face_trace, layer_data):
        side_layer, inverse_layer, jacobian_layer = layer_data
        right_load = side_layer - couple(lift_maps[0], jacobian_layer[:, 0], face_trace)
        element_value = jnp.einsum('cij,cj->ci', inverse_layer, right_load, precision=HIGHEST)
        return face_traces(element_value)[1], element_value

    zero_trace = jnp.zeros((right_side.shape[1], VARS, FACE), jnp.float32)
    carried, lower_part = lax.scan(forward, zero_trace, (right_side, inverses, jacobians))

    def backward(face_trace, layer_data):
        lower_layer, inverse_layer, jacobian_layer = layer_data
        right_load = couple(lift_maps[1], jacobian_layer[:, 1], face_trace)
        element_value = lower_layer - jnp.einsum('cij,cj->ci', inverse_layer, right_load, precision=HIGHEST)
        return face_traces(element_value)[0], element_value

    carried, upper_part = lax.scan(backward, zero_trace, (lower_part, inverses, jacobians), reverse=True)
    return upper_part


def reference(vector, inverses, lift_maps, jacobians, orient):
    solution = line_sweep(vector, inverses, lift_maps, jacobians)
    for passage in range(PASSES - 1):
        solution = line_sweep(vector - cross_load(solution, lift_maps, jacobians, orient), inverses, lift_maps, jacobians)
    return solution
```

```python
import functools

import jax
import jax.numpy as jnp
import numpy as np
from jax import lax
from jax.experimental import pallas as pl
from jax.experimental.pallas import tpu as pltpu
from jax.sharding import PartitionSpec as P

ORDER = 3
EXTENT = ORDER + 1
VARS = 5
FACE = EXTENT * EXTENT
TRACE = VARS * FACE
BLOCK = VARS * FACE * EXTENT
HALF = BLOCK // 2
SLOTS = (0, EXTENT - 1) + tuple(range(1, EXTENT - 1))
WIDE = 256
ROWS = TRACE + 8
F32 = jnp.float32
BF16 = jnp.bfloat16


def split(value):
    high = value.astype(BF16)
    return high, (value - high.astype(F32)).astype(BF16)


def product(left, right, transposed=False):
    dims = (((1,), (1 if transposed else 0,)), ((), ()))
    dot = functools.partial(lax.dot_general, dimension_numbers=dims, preferred_element_type=F32)
    left_high, left_low = left
    right_high, right_low = right
    return dot(left_high, right_high) + (dot(left_high, right_low) + dot(left_low, right_high))


def spread(value):
    wide = BLOCK - BLOCK % WIDE
    high_part, low_part = split(value)
    none = jnp.zeros((value.shape[0], WIDE - 3 * (BLOCK - wide)), BF16)
    return (high_part[:, :wide], low_part[:, :wide]), (high_part[:, wide:], low_part[:, wide:]), none


def pack_left(value):
    (body_high, body_low), (tail_high, tail_low), none = spread(value)
    return jnp.concatenate([body_high, body_high, body_low, tail_high, tail_high, tail_low, none], axis=1)


def pack_right(value):
    (body_high, body_low), (tail_high, tail_low), none = spread(value)
    return jnp.concatenate([body_high, body_low, body_high, tail_high, tail_low, tail_high, none], axis=1)


def against(left, right):
    return lax.dot_general(left, right, (((1,), (1,)), ((), ())), preferred_element_type=F32)


def faced(face, value):
    high_part, low_part = split(value)
    return jnp.dot(
        face, jnp.concatenate([high_part, low_part, high_part], axis=0), preferred_element_type=F32
    )


def multiply(left, right):
    return product(split(left), split(right))


def lanes(shape):
    return lax.broadcasted_iota(jnp.int32, shape, 1)


def rows(shape):
    return lax.broadcasted_iota(jnp.int32, shape, 0)


def keep(mask, value):
    return jnp.where(mask, value, 0.0)


def low(value):
    return keep(lanes(value.shape) < TRACE, value)


def high(value):
    lane = lanes(value.shape)
    return keep((lane >= TRACE) & (lane < 2 * TRACE), value)


def below(value):
    return jnp.concatenate([jnp.zeros((TRACE, value.shape[1]), F32), value], axis=0)


def to_low(value):
    return low(pltpu.roll(value, WIDE - 2 * TRACE, 1))


def join(left, right):
    lane = lanes((TRACE, WIDE))
    through = below(keep(lane < 2 * TRACE, right[:TRACE]))
    first = multiply(left[:, : 2 * TRACE], through)
    lane_all = lanes((ROWS, WIDE))
    row_all = rows((ROWS, WIDE))
    first = first + keep((lane_all >= 2 * TRACE) | (row_all >= TRACE), right)
    back = left[:TRACE]
    through = jnp.concatenate(
        [to_low(back), jnp.zeros((TRACE, WIDE), F32), keep(lane >= 2 * TRACE, back)], axis=0
    )
    second = multiply(first[:, : 3 * TRACE], through)
    middle = (lane_all >= TRACE) & (lane_all < 2 * TRACE)
    return first, second + keep(middle, first) + keep(lane_all < TRACE, left)


def apply(column, matrix):
    return jnp.sum(column * matrix, axis=0, keepdims=True)


def stack(parts):
    total = jnp.zeros((8, parts[0].shape[1]), F32)
    row = rows(total.shape)
    for index, part in enumerate(parts):
        total = jnp.where(row == index, jnp.broadcast_to(part, total.shape), total)
    return total


def each(z, matrices):
    pieces = split(z[:, : 2 * TRACE])
    row = rows((8, WIDE))
    total = jnp.zeros((8, WIDE), F32)
    for index, matrix in enumerate(matrices):
        total = jnp.where(row == index, product(pieces, split(matrix)), total)
    return total


def kernel(
    layers, cells, width, rounds,
    inv, vector, lift_maps, jacobians, orient, pick_source, out,
    blocks, block_sem, lifts, lift_sem, pick, pick_sem, vecs, jac_rows, packed, near,
    ends, sides, inner, full, y, x, entry, climb, reach, zmat, firsts,
    mine, theirs, send_sem, recv_sem, tail_sems, z_mine, z_theirs, z_send, z_recv,
    turns, traces, backs, got_high, got_back, from_left, from_right, cross_sems, natural,
):
    elements = layers * cells
    place = lax.axis_index("stream")
    column_at = lax.axis_index("cross")
    last = layers - 1
    vec_rows = vecs.shape[0]

    def at(layer, c):
        return layer * cells + c

    order = [at(layer, c) for c in range(cells) for layer in range(layers)]

    lift_copies = [
        pltpu.make_async_copy(lift_maps.at[2 * h : 2 * h + 2], lifts.at[2 * h : 2 * h + 2], lift_sem.at[h])
        for h in range(2)
    ]

    def block_copies(e, slots):
        return [
            pltpu.make_async_copy(inv.at[e, :, SLOTS[s]], blocks.at[e, s], block_sem.at[e, s]) for s in slots
        ]

    early, late = (0, 1), tuple(range(2, EXTENT))
    lift_copies[0].start()
    for e in order:
        for copy in block_copies(e, early):
            copy.start()
    pick_copy = pltpu.make_async_copy(pick_source, pick, pick_sem.at[0])

    bits = [lax.rem(place // (1 << k), 2) for k in range(rounds)]
    partners = [place + (1 - 2 * bits[k]) * (1 << k) for k in range(rounds)]
    barrier = pltpu.get_barrier_semaphore()
    for k in range(rounds):
        pl.semaphore_signal(barrier, inc=1, device_id=(partners[k], column_at), device_id_type=pl.DeviceIdType.MESH)

    @pl.when(column_at > 0)
    def _():
        pl.semaphore_signal(barrier, inc=1, device_id=(place, column_at - 1), device_id_type=pl.DeviceIdType.MESH)

    @pl.when(column_at < width - 1)
    def _():
        pl.semaphore_signal(barrier, inc=1, device_id=(place, column_at + 1), device_id_type=pl.DeviceIdType.MESH)

    vecs[...] = jnp.zeros_like(vecs)
    jac_rows[...] = jnp.zeros_like(jac_rows)
    for e in range(elements):
        vecs[e : e + 1, :] = vector[e // cells, e % cells : e % cells + 1, :]
        for v in range(VARS):
            for w in range(VARS):
                jac_rows[e, w, :4, v * FACE : (v + 1) * FACE] = jacobians[e, v, w]
        for w in range(VARS):
            value = jac_rows[e, w]
            jac_rows[e, w] = value + pltpu.roll(value, TRACE, 1) + pltpu.roll(value, 2 * TRACE, 1)
    ends[...] = jnp.zeros_like(ends)
    sides[...] = jnp.zeros_like(sides)
    y[...] = jnp.zeros_like(y)
    backs[...] = jnp.zeros_like(backs)

    row_face = rows((TRACE, TRACE))
    lane_face = lanes((TRACE, TRACE))
    row_wide = lax.rem(rows((TRACE, WIDE)), FACE)
    lane_wide = lax.rem(lanes((TRACE, WIDE)), FACE)
    same = row_wide == lane_wide
    leading = lanes((TRACE, WIDE)) < 2 * TRACE
    eye = rows((TRACE, WIDE)) == lanes((TRACE, WIDE))
    eye_low = eye.astype(F32)
    eye_high = (rows((TRACE, WIDE)) + TRACE == lanes((TRACE, WIDE))).astype(F32)
    first_row = rows((8, WIDE)) == 0

    def source_of(code, node_index):
        first = lax.div(node_index, EXTENT)
        second = node_index - first * EXTENT
        first, second = (
            first + lax.rem(code, 2) * (second - first),
            second + lax.rem(code, 2) * (first - second),
        )
        first = first + lax.rem(code // 2, 2) * (EXTENT - 1 - 2 * first)
        second = second + lax.rem(code // 4, 2) * (EXTENT - 1 - 2 * second)
        return first * EXTENT + second

    def face(e, m, chosen):
        tall = jnp.concatenate(
            [jnp.broadcast_to(jac_rows[e, w, m : m + 1, :], (FACE, WIDE)) for w in range(VARS)],
            axis=0,
        )
        value = keep(chosen, tall)
        value = jnp.where(leading, value, value - value.astype(BF16).astype(F32))
        return value[:, : 3 * TRACE].astype(BF16)

    def half(e, h):
        return pack_right(blocks[e, 2 * h : 2 * h + 2].reshape(HALF, BLOCK))

    def ending(e, h, through):
        ends[e, h, TRACE:, :HALF] = -faced(face(e, 0, same), through[:TRACE])
        ends[e, h, :TRACE, :HALF] = -faced(face(e, 1, same), through[TRACE : 2 * TRACE])

    vec_at, rest_at = 2 * TRACE, 2 * TRACE + vec_rows
    packed[vec_at:rest_at] = pack_left(vecs[...])
    lift_copies[0].wait()
    packed[:vec_at] = pack_left(lifts[0:2].reshape(2 * TRACE, BLOCK))

    def critical(e):
        block = half(e, 0)
        near[e] = block
        through = against(packed[:rest_at], block)
        y[0, e : e + 1, :HALF] = through[vec_at + e : vec_at + e + 1]
        ending(e, 0, through)

    def rest(e):
        through = against(packed[...], half(e, 1))
        y[1, e : e + 1, :HALF] = through[vec_at + e : vec_at + e + 1]
        ending(e, 1, through)
        chosen = row_wide == source_of(orient[e % cells, e // cells], lane_wide)
        faces = face(e, 2, chosen), face(e, 3, same)
        for h, value in enumerate((against(packed[rest_at:], near[e]), through[rest_at:])):
            for m in range(2):
                sides[e, h, m * TRACE : (m + 1) * TRACE, :HALF] = faced(
                    faces[m], value[m * TRACE : (m + 1) * TRACE]
                )

    def finish(e):
        for h in range(2):
            full[e, h] = product(split(inner[e, :, : 2 * TRACE]), split(ends[e, h]))

    def chain(c):
        up = [ends[at(layer, c), 0, TRACE:] for layer in range(layers)]
        down = [ends[at(layer, c), 0, :TRACE] for layer in range(layers)]

        def bottom(layer):
            e = at(layer, c)
            return keep(first_row, jnp.broadcast_to(y[0, e : e + 1, :], (8, WIDE)))

        forward = [jnp.concatenate([up[0], bottom(0)], axis=0)]
        for layer in range(1, layers):
            step = multiply(forward[-1][:, : 2 * TRACE], below(up[layer]))
            forward.append(step + below(bottom(layer)))
            yield
        none = jnp.zeros((ROWS, WIDE), F32)
        backward = jnp.concatenate([eye_low, none], axis=0)
        for layer in reversed(range(layers)):
            before = forward[layer - 1] if layer else jnp.concatenate([eye_high, none[TRACE:]], axis=0)
            inner[at(layer, c)] = backward + below(high(before))
            if layer == last:
                backward = low(jnp.concatenate([down[layer], forward[layer]], axis=0))
            else:
                backward = low(multiply(backward[:, :TRACE], down[layer]) + below(forward[layer]))
                yield
        whole = backward[TRACE:] + high(forward[last])
        extra = pltpu.roll(backward[:TRACE], 2 * TRACE, 1)
        mine[0, c, TRACE:] = whole[TRACE:]
        mine[0, c, :TRACE] = whole[:TRACE] + extra

    def responses(c):
        behind = eye_low
        reach_low, after = [], []
        for layer in range(layers):
            reach_low.append(behind)
            e = at(layer, c)
            pair = jnp.concatenate([ends[e, 0, TRACE:], ends[e, 0, :TRACE]], axis=0)
            if layer == 0:
                both = low(pair)
            else:
                both = low(multiply(pair[:, :TRACE], behind))
            after.append(both[:TRACE])
            behind = both[TRACE:]
        ahead = eye_high
        for layer in reversed(range(layers)):
            e = at(layer, c)
            zmat[e, :TRACE] = reach_low[layer]
            zmat[e, TRACE:] = ahead
            if layer:
                if layer == last:
                    ahead = high(ends[e, 0, TRACE:]) + after[layer]
                else:
                    ahead = multiply(ends[e, 0, TRACE:, : 2 * TRACE], below(ahead)) + after[layer]

    def ordered(k, c):
        flag = bits[k] == 1
        ours, other = mine[k, c], theirs[k, c]
        return jnp.where(flag, other, ours), jnp.where(flag, ours, other)

    def reaching(k, c, first):
        flag = bits[k] == 1
        if k == 0:
            near, far = eye_low, low(first)
            ahead = eye_high
        else:
            near, ahead = entry[c, :TRACE], entry[c, TRACE : 2 * TRACE]
            far = multiply(first[:, :TRACE], near)
        reach[k, c, :TRACE] = jnp.where(flag, 0.0, near)
        reach[k, c, TRACE:] = jnp.where(flag, ahead, far)

    def level(k, c):
        left, right = ordered(k, c)
        reaching(k, c, right[:TRACE])
        flag = bits[k] == 1
        first = firsts[k, c]
        step = jnp.concatenate(
            [
                jnp.where(flag, eye_low, to_low(right[:TRACE])),
                jnp.where(flag, high(left[:TRACE]), low(first[:TRACE]) + eye_high),
                jnp.where(flag, high(left[TRACE:]), low(first[TRACE:])),
            ],
            axis=0,
        )
        if k == 0:
            entry[c] = step
        else:
            old = entry[c]
            moved = multiply(step[:, : 2 * TRACE], old[: 2 * TRACE])
            entry[c, : 2 * TRACE] = moved[: 2 * TRACE]
            entry[c, 2 * TRACE :] = moved[2 * TRACE :] + old[2 * TRACE :]
        back = to_low(left[:TRACE])
        climb[k, c, :TRACE] = back
        climb[k, c, TRACE:] = multiply(right[:TRACE, :TRACE], back) + high(right[:TRACE])

    block_row, block_lane = lax.div(row_face, FACE), lax.div(lane_face, FACE)
    face_lane = lane_face - block_lane * FACE

    def turn(e):
        within = row_face - block_row * FACE
        chosen = (block_row == block_lane) & (source_of(orient[e % cells, e // cells], within) == face_lane)
        turns[e] = chosen.astype(F32)

    def remote(source, target, send, recv, device):
        return pltpu.make_async_remote_copy(
            src_ref=source, dst_ref=target, send_sem=send, recv_sem=recv,
            device_id=device, device_id_type=pl.DeviceIdType.MESH,
        )

    sent = []
    pending = {}

    def dispatch(k, c):
        device = (partners[k], column_at)
        send, recv = send_sem.at[k, c], recv_sem.at[k, c]
        if k < rounds - 1:
            pending[k, c] = [remote(mine.at[k, c], theirs.at[k, c], send, recv, device)]
        else:
            one, two = pl.ds(0, 128), pl.ds(128, 128)
            foot = pl.ds(TRACE, 8)
            pending[k, c] = [
                remote(mine.at[k, c, :, one], theirs.at[k, c, :, one], send, recv, device),
                remote(
                    mine.at[k, c, foot, two], theirs.at[k, c, foot, two],
                    tail_sems.at[0, c], tail_sems.at[1, c], device,
                ),
            ]
        for copy in pending[k, c]:
            copy.start()
            sent.append(copy)

    sides_met = jnp.minimum(column_at, 1) + jnp.minimum(width - 1 - column_at, 1)
    def column_of(c):
        return [at(layer, c) for layer in range(layers)]

    def ready(members, slots):
        for e in members:
            for copy in block_copies(e, slots):
                copy.wait()

    ready(column_of(0), early)
    lift_copies[1].start()
    for e in order:
        for copy in block_copies(e, late):
            copy.start()
    pick_copy.start()
    for e in column_of(0):
        critical(e)
    for c in range(cells):
        steps = chain(c)
        if c + 1 < cells:
            ready(column_of(c + 1), early)
            for e in column_of(c + 1):
                next(steps, None)
                critical(e)
        for _ in steps:
            pass
        if c == 0:
            pl.semaphore_wait(barrier, rounds + sides_met)
        dispatch(0, c)

    lift_copies[1].wait()
    packed[rest_at:] = pack_left(lifts[2:4].reshape(2 * TRACE, BLOCK))
    ready(order, late)
    if rounds == 1:
        for c in range(cells):
            entry[c] = jnp.concatenate([eye_low, eye_high, jnp.zeros((8, WIDE), F32)], axis=0)

    tasks = []
    for index, e in enumerate(order):
        tasks.append(functools.partial(rest, e))
        if index:
            tasks.append(functools.partial(finish, order[index - 1]))
    tasks.append(functools.partial(finish, order[-1]))
    for e in range(elements):
        tasks.append(functools.partial(turn, e))
    for c in range(cells):
        tasks.append(functools.partial(responses, c))

    slots = rounds * cells
    quota = -(-len(tasks) // slots)

    def work(count):
        for _ in range(min(count, len(tasks))):
            tasks.pop(0)()

    for k in range(rounds):
        for c in range(cells):
            work(quota)
            for copy in pending[k, c]:
                copy.wait_recv()
            if k < rounds - 1:
                left, right = ordered(k, c)
                first, node = join(left, right)
                mine[k + 1, c] = node
                dispatch(k + 1, c)
                firsts[k, c] = first
                level(k, c)
    work(len(tasks))

    top = rounds - 1
    top_flag = bits[top] == 1

    def meet(z_ours, z_other, flag):
        z_left, z_right = jnp.where(flag, z_other, z_ours), jnp.where(flag, z_ours, z_other)
        return low(z_right) + high(z_left), low(z_left) + high(z_right)

    z_ours = stack([mine[top, c, TRACE : TRACE + 1] for c in range(cells)])
    z_other = stack([theirs[top, c, TRACE : TRACE + 1] for c in range(cells)])
    met, _ = meet(z_ours, z_other, top_flag)
    turned = each(met, [below(low(theirs[top, c, :TRACE])) for c in range(cells)])
    arrived = jnp.where(top_flag, high(met), low(met + turned))
    z_in = each(arrived, [entry[c, : 2 * TRACE] for c in range(cells)]) + stack(
        [entry[c, 2 * TRACE : 2 * TRACE + 1] for c in range(cells)]
    )
    column = z_in.T
    for layer in range(layers):
        for c in range(cells):
            e = at(layer, c)
            for h in range(2):
                x[h, e : e + 1, :] = (
                    y[h, e : e + 1, :]
                    + full[e, h, 2 * TRACE : 2 * TRACE + 1]
                    + apply(column[: 2 * TRACE, c : c + 1], full[e, h, : 2 * TRACE])
                )

    pick_copy.wait()
    cross = jnp.zeros((elements, WIDE), F32)
    for h in range(2):
        x_high, x_low = split(x[h])
        cross = cross + (
            jnp.dot(x_high, pick[h], preferred_element_type=F32)
            + jnp.dot(x_low, pick[h], preferred_element_type=F32)
        )
    traces[...] = cross[:, 128:]
    column = cross[:, :128].T
    for e in range(elements):
        backs[e : e + 1, :TRACE] = apply(column[:TRACE, e : e + 1], turns[e])
    up = remote(traces, got_high, cross_sems.at[0], cross_sems.at[1], (place, lax.rem(column_at + 1, width)))
    down = remote(backs, got_back, cross_sems.at[2], cross_sems.at[3], (place, lax.rem(column_at + width - 1, width)))

    @pl.when(column_at < width - 1)
    def _():
        up.start()

    @pl.when(column_at > 0)
    def _():
        down.start()

    for c in range(cells):
        reaching(top, c, jnp.concatenate([theirs[top, c, :TRACE, :128], jnp.zeros((TRACE, WIDE - 128), F32)], axis=1))
    for layer in range(layers):
        for c in range(cells):
            e = at(layer, c)
            if c > 0:
                from_left[e : e + 1, :] = traces[e - 1 : e, :]
            if c < cells - 1:
                from_right[e : e + 1, :] = backs[e + 1 : e + 2, :]
    firsts_at = [layer * cells for layer in range(layers)]
    lasts_at = [layer * cells + cells - 1 for layer in range(layers)]

    @pl.when(column_at > 0)
    def _():
        up.wait_recv()
        for one, two in zip(firsts_at, lasts_at):
            from_left[one : one + 1, :] = got_high[two : two + 1, :]

    @pl.when(column_at == 0)
    def _():
        for one in firsts_at:
            from_left[one : one + 1, :] = jnp.zeros((1, 128), F32)

    @pl.when(column_at < width - 1)
    def _():
        down.wait_recv()
        for one, two in zip(firsts_at, lasts_at):
            from_right[two : two + 1, :] = got_back[one : one + 1, :]

    @pl.when(column_at == width - 1)
    def _():
        for two in lasts_at:
            from_right[two : two + 1, :] = jnp.zeros((1, 128), F32)

    left_columns = from_left[...].T
    right_columns = from_right[...].T

    def loaded(e, h):
        return y[h, e : e + 1, :] - (
            apply(left_columns[:TRACE, e : e + 1], sides[e, h, :TRACE])
            + apply(right_columns[:TRACE, e : e + 1], sides[e, h, TRACE:])
        )

    for e in range(elements):
        y[0, e : e + 1, :] = loaded(e, 0)
    columns = y[0].T
    z_mine[0] = stack([
        functools.reduce(
            jnp.add,
            [apply(columns[: 2 * TRACE, at(layer, c) : at(layer, c) + 1], zmat[at(layer, c)]) for layer in range(layers)],
        )
        for c in range(cells)
    ])

    state = {}

    def gathered(layer):
        return stack([y[0, at(layer, c) : at(layer, c) + 1, :] for c in range(cells)])

    def local_sweeps():
        forward = [gathered(0)]
        for layer in range(1, layers):
            step = each(forward[-1], [below(ends[at(layer, c), 0, TRACE:]) for c in range(cells)])
            forward.append(step + gathered(layer))
        backward = jnp.zeros((8, WIDE), F32)
        for layer in reversed(range(layers)):
            before = high(forward[layer - 1]) if layer else jnp.zeros((8, WIDE), F32)
            state[layer] = backward + before
            if layer == last:
                backward = low(forward[layer])
            elif layer:
                inverse = [
                    jnp.concatenate([ends[at(layer, c), 0, :TRACE], jnp.zeros((TRACE, WIDE), F32)], axis=0)
                    for c in range(cells)
                ]
                backward = low(each(backward, inverse) + forward[layer])

    def local_rest():
        for e in range(elements):
            y[1, e : e + 1, :] = loaded(e, 1)

    def local_apply():
        for layer in range(layers):
            column = state[layer].T
            for c in range(cells):
                e = at(layer, c)
                for h in range(2):
                    x[h, e : e + 1, :] = y[h, e : e + 1, :] + apply(column[: 2 * TRACE, c : c + 1], ends[e, h])

    tasks = [local_sweeps, local_rest, local_apply]
    z_in = jnp.zeros((8, WIDE), F32)
    for k in range(rounds):
        flag = bits[k] == 1
        copy = remote(z_mine.at[k], z_theirs.at[k], z_send.at[k], z_recv.at[k], (partners[k], column_at))
        copy.start()
        sent.append(copy)
        if k < rounds - 1:
            work(1)
        else:
            work(len(tasks))
        copy.wait_recv()
        met, kept = meet(z_mine[k], z_theirs[k], flag)
        if k < rounds - 1:
            z_mine[k + 1] = each(met, [climb[k, c] for c in range(cells)]) + kept
        z_in = z_in + each(met, [reach[k, c] for c in range(cells)])

    column = z_in.T
    for layer in range(layers):
        for c in range(cells):
            e = at(layer, c)
            for h in range(2):
                x[h, e : e + 1, :] = x[h, e : e + 1, :] + apply(
                    column[: 2 * TRACE, c : c + 1], full[e, h, : 2 * TRACE]
                )
    for slot, i in enumerate(SLOTS):
        for v in range(VARS):
            target = (v * EXTENT + i) * FACE
            source = (slot % 2) * TRACE + v * FACE
            natural[:, target : target + FACE] = x[slot // 2, :, source : source + FACE]
    for layer in range(layers):
        out[layer] = natural[layer * cells : (layer + 1) * cells, :]

    for copy in sent:
        copy.wait_send()

    @pl.when(column_at < width - 1)
    def _():
        up.wait_send()

    @pl.when(column_at > 0)
    def _():
        down.wait_send()


def picker():
    table = np.zeros((2, WIDE, WIDE), np.float32)
    for slot, i in enumerate(SLOTS):
        for v in range(VARS):
            for k in range(EXTENT):
                source = (slot % 2) * TRACE + v * FACE + k
                target = v * FACE + i * EXTENT + k
                table[slot // 2, source, target] = 1.0
                table[slot // 2, source + (EXTENT - 1) * EXTENT, 128 + target] = 1.0
    return table


def on_device(width, count, vector, inverses, lift_maps, jacobians, orient):
    layers, cells = vector.shape[:2]
    elements = layers * cells
    rounds = count.bit_length() - 1
    inv = inverses.reshape(elements, VARS, EXTENT, FACE, BLOCK)
    flat = jacobians.transpose(0, 1, 3, 4, 2, 5).reshape(elements, VARS, VARS, 4, FACE)
    pick = jnp.asarray(picker(), BF16)
    vec_rows = -(-elements // 16) * 16
    depth = 4 * TRACE + vec_rows
    vmem = pl.BlockSpec(memory_space=pltpu.VMEM)
    hbm = pl.BlockSpec(memory_space=pltpu.HBM)
    tall = 2 * TRACE + 8
    result = pl.pallas_call(
        functools.partial(kernel, layers, cells, width, rounds),
        out_shape=jax.ShapeDtypeStruct((layers, cells, BLOCK), F32),
        in_specs=[hbm, vmem, hbm, vmem, pl.BlockSpec(memory_space=pltpu.SMEM), hbm],
        out_specs=vmem,
        scratch_shapes=[
            pltpu.VMEM((elements, EXTENT, VARS, FACE, BLOCK), F32),
            pltpu.SemaphoreType.DMA((elements, EXTENT)),
            pltpu.VMEM((4, TRACE, BLOCK), F32),
            pltpu.SemaphoreType.DMA((2,)),
            pltpu.VMEM((2, WIDE, WIDE), BF16),
            pltpu.SemaphoreType.DMA((1,)),
            pltpu.VMEM((vec_rows, BLOCK), F32),
            pltpu.VMEM((elements, VARS, 8, WIDE), F32),
            pltpu.VMEM((depth, 4 * WIDE), BF16),
            pltpu.VMEM((elements, HALF, 4 * WIDE), BF16),
            pltpu.VMEM((elements, 2, 2 * TRACE, WIDE), F32),
            pltpu.VMEM((elements, 2, 2 * TRACE, WIDE), F32),
            pltpu.VMEM((elements, tall, WIDE), F32),
            pltpu.VMEM((elements, 2, tall, WIDE), F32),
            pltpu.VMEM((2, elements, WIDE), F32),
            pltpu.VMEM((2, elements, WIDE), F32),
            pltpu.VMEM((cells, tall, WIDE), F32),
            pltpu.VMEM((rounds, cells, 2 * TRACE, WIDE), F32),
            pltpu.VMEM((rounds, cells, 2 * TRACE, WIDE), F32),
            pltpu.VMEM((elements, 2 * TRACE, WIDE), F32),
            pltpu.VMEM((rounds, cells, ROWS, WIDE), F32),
            pltpu.VMEM((rounds, cells, ROWS, WIDE), F32),
            pltpu.VMEM((rounds, cells, ROWS, WIDE), F32),
            pltpu.SemaphoreType.DMA((rounds, cells)),
            pltpu.SemaphoreType.DMA((rounds, cells)),
            pltpu.SemaphoreType.DMA((2, cells)),
            pltpu.VMEM((rounds, 8, WIDE), F32),
            pltpu.VMEM((rounds, 8, WIDE), F32),
            pltpu.SemaphoreType.DMA((rounds,)),
            pltpu.SemaphoreType.DMA((rounds,)),
            pltpu.VMEM((elements, TRACE, TRACE), F32),
            pltpu.VMEM((elements, 128), F32),
            pltpu.VMEM((elements, 128), F32),
            pltpu.VMEM((elements, 128), F32),
            pltpu.VMEM((elements, 128), F32),
            pltpu.VMEM((elements, 128), F32),
            pltpu.VMEM((elements, 128), F32),
            pltpu.SemaphoreType.DMA((4,)),
            pltpu.VMEM((elements, BLOCK), F32),
        ],
        compiler_params=pltpu.CompilerParams(
            collective_id=0, has_side_effects=True, vmem_limit_bytes=62 * 1024 * 1024
        ),
    )(inv, vector, lift_maps.transpose(0, 2, 1), flat, orient.T, pick)
    return result


def solution(mesh):
    in_specs = (
        P("stream", "cross", None),
        P("stream", "cross", None, None),
        P(),
        P("stream", "cross", None, None, None, None),
        P("stream", "cross"),
    )
    out_specs = P("stream", "cross", None)
    return jax.shard_map(
        functools.partial(on_device, mesh.shape["cross"], mesh.shape["stream"]),
        mesh=mesh, in_specs=in_specs, out_specs=out_specs, check_vma=False,
    )
```

```python
import functools

import jax
import jax.numpy as jnp
import numpy as np
from jax import lax
from jax.experimental import pallas as pl
from jax.experimental.pallas import tpu as pltpu
from jax.sharding import PartitionSpec as P

ORDER = 3
EXTENT = ORDER + 1
VARS = 5
FACE = EXTENT * EXTENT
TRACE = VARS * FACE
BLOCK = VARS * FACE * EXTENT
HALF = BLOCK // 2
SLOTS = (0, EXTENT - 1) + tuple(range(1, EXTENT - 1))
WIDE = 256
ROWS = TRACE + 8
BUDGETS = (1.7, 1.0)
F32 = jnp.float32
BF16 = jnp.bfloat16


def split(value):
    high = value.astype(BF16)
    return high, (value - high.astype(F32)).astype(BF16)


def product(left, right, transposed=False):
    dims = (((1,), (1 if transposed else 0,)), ((), ()))
    dot = functools.partial(lax.dot_general, dimension_numbers=dims, preferred_element_type=F32)
    left_high, left_low = left
    right_high, right_low = right
    return dot(left_high, right_high) + (dot(left_high, right_low) + dot(left_low, right_high))


def spread(value):
    wide = BLOCK - BLOCK % WIDE
    high_part, low_part = split(value)
    none = jnp.zeros((value.shape[0], WIDE - 3 * (BLOCK - wide)), BF16)
    return (high_part[:, :wide], low_part[:, :wide]), (high_part[:, wide:], low_part[:, wide:]), none


def pack_left(value):
    (body_high, body_low), (tail_high, tail_low), none = spread(value)
    return jnp.concatenate([body_high, body_high, body_low, tail_high, tail_high, tail_low, none], axis=1)


def pack_right(value):
    (body_high, body_low), (tail_high, tail_low), none = spread(value)
    return jnp.concatenate([body_high, body_low, body_high, tail_high, tail_low, tail_high, none], axis=1)


def against(left, right):
    return lax.dot_general(left, right, (((1,), (1,)), ((), ())), preferred_element_type=F32)


def faced(face, value):
    high_part, low_part = split(value)
    return jnp.dot(
        face, jnp.concatenate([high_part, low_part, high_part], axis=0), preferred_element_type=F32
    )


def multiply(left, right):
    return product(split(left), split(right))


def lanes(shape):
    return lax.broadcasted_iota(jnp.int32, shape, 1)


def rows(shape):
    return lax.broadcasted_iota(jnp.int32, shape, 0)


def keep(mask, value):
    return jnp.where(mask, value, 0.0)


def low(value):
    return keep(lanes(value.shape) < TRACE, value)


def high(value):
    lane = lanes(value.shape)
    return keep((lane >= TRACE) & (lane < 2 * TRACE), value)


def below(value):
    return jnp.concatenate([jnp.zeros((TRACE, value.shape[1]), F32), value], axis=0)


def to_low(value):
    return low(pltpu.roll(value, WIDE - 2 * TRACE, 1))


def join(left, right):
    lane = lanes((TRACE, WIDE))
    through = below(keep(lane < 2 * TRACE, right[:TRACE]))
    first = multiply(left[:, : 2 * TRACE], through)
    lane_all = lanes((ROWS, WIDE))
    row_all = rows((ROWS, WIDE))
    first = first + keep((lane_all >= 2 * TRACE) | (row_all >= TRACE), right)
    back = left[:TRACE]
    through = jnp.concatenate(
        [to_low(back), jnp.zeros((TRACE, WIDE), F32), keep(lane >= 2 * TRACE, back)], axis=0
    )
    second = multiply(first[:, : 3 * TRACE], through)
    middle = (lane_all >= TRACE) & (lane_all < 2 * TRACE)
    return first, second + keep(middle, first) + keep(lane_all < TRACE, left)


def apply(column, matrix):
    return jnp.sum(column * matrix, axis=0, keepdims=True)


def stack(parts):
    total = jnp.zeros((8, parts[0].shape[1]), F32)
    row = rows(total.shape)
    for index, part in enumerate(parts):
        total = jnp.where(row == index, jnp.broadcast_to(part, total.shape), total)
    return total


def each(z, matrices):
    pieces = split(z[:, : 2 * TRACE])
    row = rows((8, WIDE))
    total = jnp.zeros((8, WIDE), F32)
    for index, matrix in enumerate(matrices):
        total = jnp.where(row == index, product(pieces, split(matrix)), total)
    return total


def kernel(
    layers, cells, width, rounds,
    inv, vector_source, lift_maps, jacobian_source, orient, pick_source, out,
    blocks, block_sem, lifts, lift_sem, pick, pick_sem, vector, jacobians, input_sem, vecs, jac_rows, packed, near,
    ends, sides, inner, full, y, x, entry, climb, reach, zmat, firsts,
    mine, theirs, send_sem, recv_sem, tail_sems, z_mine, z_theirs, z_send, z_recv,
    turns, traces, backs, got_high, got_back, from_left, from_right, cross_sems, natural,
):
    elements = layers * cells
    place = lax.axis_index("stream")
    column_at = lax.axis_index("cross")
    last = layers - 1
    vec_rows = vecs.shape[0]

    def at(layer, c):
        return layer * cells + c

    order = [at(layer, c) for c in range(cells) for layer in range(layers)]

    lift_copies = [
        pltpu.make_async_copy(lift_maps.at[2 * h : 2 * h + 2], lifts.at[2 * h : 2 * h + 2], lift_sem.at[h])
        for h in range(2)
    ]

    def block_copies(e, slots):
        return [
            pltpu.make_async_copy(inv.at[e, :, SLOTS[s]], blocks.at[e, s], block_sem.at[e, s]) for s in slots
        ]

    early, late = (0, 1), tuple(range(2, EXTENT))
    def column_of(c):
        return [at(layer, c) for layer in range(layers)]

    def fetch(members, slots):
        for e in members:
            for copy in block_copies(e, slots):
                copy.start()

    def ready(members, slots):
        for e in members:
            for copy in block_copies(e, slots):
                copy.wait()

    input_copies = [
        pltpu.make_async_copy(jacobian_source, jacobians, input_sem.at[0]),
        pltpu.make_async_copy(vector_source, vector, input_sem.at[1]),
    ]
    input_copies[1].start()
    lift_copies[0].start()
    fetch(column_of(0), early)
    input_copies[0].start()
    pick_copy = pltpu.make_async_copy(pick_source, pick, pick_sem.at[0])

    bits = [lax.rem(place // (1 << k), 2) for k in range(rounds)]
    partners = [place + (1 - 2 * bits[k]) * (1 << k) for k in range(rounds)]
    barrier = pltpu.get_barrier_semaphore()
    for k in range(rounds):
        pl.semaphore_signal(barrier, inc=1, device_id=(partners[k], column_at), device_id_type=pl.DeviceIdType.MESH)

    @pl.when(column_at > 0)
    def _():
        pl.semaphore_signal(barrier, inc=1, device_id=(place, column_at - 1), device_id_type=pl.DeviceIdType.MESH)

    @pl.when(column_at < width - 1)
    def _():
        pl.semaphore_signal(barrier, inc=1, device_id=(place, column_at + 1), device_id_type=pl.DeviceIdType.MESH)

    vecs[...] = jnp.zeros_like(vecs)
    jac_rows[...] = jnp.zeros_like(jac_rows)
    backs[...] = jnp.zeros_like(backs)

    def spread_jacobians(c):
        for e in column_of(c):
            for v in range(VARS):
                for w in range(VARS):
                    jac_rows[e, w, :4, v * FACE : (v + 1) * FACE] = jacobians[e, v, w]
            for w in range(VARS):
                value = jac_rows[e, w]
                jac_rows[e, w] = value + pltpu.roll(value, TRACE, 1) + pltpu.roll(value, 2 * TRACE, 1)

    input_copies[1].wait()
    for e in range(elements):
        vecs[e : e + 1, :] = vector[e // cells, e % cells : e % cells + 1, :]

    row_face = rows((TRACE, TRACE))
    lane_face = lanes((TRACE, TRACE))
    row_wide = lax.rem(rows((TRACE, WIDE)), FACE)
    lane_wide = lax.rem(lanes((TRACE, WIDE)), FACE)
    same = row_wide == lane_wide
    leading = lanes((TRACE, WIDE)) < 2 * TRACE
    eye = rows((TRACE, WIDE)) == lanes((TRACE, WIDE))
    eye_low = eye.astype(F32)
    eye_high = (rows((TRACE, WIDE)) + TRACE == lanes((TRACE, WIDE))).astype(F32)
    first_row = rows((8, WIDE)) == 0

    def source_of(code, node_index):
        first = lax.div(node_index, EXTENT)
        second = node_index - first * EXTENT
        first, second = (
            first + lax.rem(code, 2) * (second - first),
            second + lax.rem(code, 2) * (first - second),
        )
        first = first + lax.rem(code // 2, 2) * (EXTENT - 1 - 2 * first)
        second = second + lax.rem(code // 4, 2) * (EXTENT - 1 - 2 * second)
        return first * EXTENT + second

    def face(e, m, chosen):
        tall = jnp.concatenate(
            [jnp.broadcast_to(jac_rows[e, w, m : m + 1, :], (FACE, WIDE)) for w in range(VARS)],
            axis=0,
        )
        value = keep(chosen, tall)
        value = jnp.where(leading, value, value - value.astype(BF16).astype(F32))
        return value[:, : 3 * TRACE].astype(BF16)

    def half(e, h):
        return pack_right(blocks[e, 2 * h : 2 * h + 2].reshape(HALF, BLOCK))

    def ending(e, h, through):
        ends[e, h, TRACE:, :HALF] = -faced(face(e, 0, same), through[:TRACE])
        ends[e, h, :TRACE, :HALF] = -faced(face(e, 1, same), through[TRACE : 2 * TRACE])

    vec_at, rest_at = 2 * TRACE, 2 * TRACE + vec_rows
    packed[vec_at:rest_at] = pack_left(vecs[...])
    lift_copies[0].wait()
    packed[:vec_at] = pack_left(lifts[0:2].reshape(2 * TRACE, BLOCK))

    def passing(e):
        block = half(e, 0)
        near[e] = block
        through = against(packed[:rest_at], block)
        y[0, e : e + 1, :HALF] = through[vec_at + e : vec_at + e + 1]
        return through

    def rest(e):
        through = against(packed[...], half(e, 1))
        y[1, e : e + 1, :HALF] = through[vec_at + e : vec_at + e + 1]
        ending(e, 1, through)
        chosen = row_wide == source_of(orient[e % cells, e // cells], lane_wide)
        faces = face(e, 2, chosen), face(e, 3, same)
        for h, value in enumerate((against(packed[rest_at:], near[e]), through[rest_at:])):
            for m in range(2):
                sides[e, h, m * TRACE : (m + 1) * TRACE, :HALF] = faced(
                    faces[m], value[m * TRACE : (m + 1) * TRACE]
                )

    def finish(e):
        for h in range(2):
            full[e, h] = product(split(inner[e, :, : 2 * TRACE]), split(ends[e, h]))

    def chain(c):
        up = [ends[at(layer, c), 0, TRACE:] for layer in range(layers)]
        down = [ends[at(layer, c), 0, :TRACE] for layer in range(layers)]

        def bottom(layer):
            e = at(layer, c)
            return keep(first_row, jnp.broadcast_to(y[0, e : e + 1, :], (8, WIDE)))

        forward = [jnp.concatenate([up[0], bottom(0)], axis=0)]
        for layer in range(1, layers):
            step = multiply(forward[-1][:, : 2 * TRACE], below(up[layer]))
            forward.append(step + below(bottom(layer)))
            yield
        none = jnp.zeros((ROWS, WIDE), F32)
        backward = jnp.concatenate([eye_low, none], axis=0)
        for layer in reversed(range(layers)):
            before = forward[layer - 1] if layer else jnp.concatenate([eye_high, none[TRACE:]], axis=0)
            inner[at(layer, c)] = backward + below(high(before))
            if layer == last:
                backward = low(jnp.concatenate([down[layer], forward[layer]], axis=0))
            else:
                backward = low(multiply(backward[:, :TRACE], down[layer]) + below(forward[layer]))
                yield
        whole = backward[TRACE:] + high(forward[last])
        extra = pltpu.roll(backward[:TRACE], 2 * TRACE, 1)
        mine[0, c, TRACE:] = whole[TRACE:]
        mine[0, c, :TRACE] = whole[:TRACE] + extra

    def responses(c):
        behind = eye_low
        reach_low, after = [], []
        for layer in range(layers):
            reach_low.append(behind)
            e = at(layer, c)
            pair = jnp.concatenate([ends[e, 0, TRACE:], ends[e, 0, :TRACE]], axis=0)
            if layer == 0:
                both = low(pair)
            else:
                both = low(multiply(pair[:, :TRACE], behind))
                yield
            after.append(both[:TRACE])
            behind = both[TRACE:]
        ahead = eye_high
        for layer in reversed(range(layers)):
            e = at(layer, c)
            zmat[e, :TRACE] = reach_low[layer]
            zmat[e, TRACE:] = ahead
            if layer:
                if layer == last:
                    ahead = high(ends[e, 0, TRACE:]) + after[layer]
                else:
                    ahead = multiply(ends[e, 0, TRACE:, : 2 * TRACE], below(ahead)) + after[layer]
                    yield

    def ordered(k, c):
        flag = bits[k] == 1
        ours, other = mine[k, c], theirs[k, c]
        return jnp.where(flag, other, ours), jnp.where(flag, ours, other)

    def reaching(k, c, first):
        flag = bits[k] == 1
        if k == 0:
            near, far = eye_low, low(first)
            ahead = eye_high
        else:
            near, ahead = entry[k, c, :TRACE], entry[k, c, TRACE : 2 * TRACE]
            far = multiply(first[:, :TRACE], near)
        reach[k, c, :TRACE] = jnp.where(flag, 0.0, near)
        reach[k, c, TRACE:] = jnp.where(flag, ahead, far)

    def reach_level(k, c):
        other = jnp.where(bits[k] == 1, mine[k, c, :TRACE, :128], theirs[k, c, :TRACE, :128])
        reaching(k, c, jnp.concatenate([other, jnp.zeros((TRACE, WIDE - 128), F32)], axis=1))

    def level(k, c):
        left, right = ordered(k, c)
        flag = bits[k] == 1
        first = firsts[k, c]
        step = jnp.concatenate(
            [
                jnp.where(flag, eye_low, to_low(right[:TRACE])),
                jnp.where(flag, high(left[:TRACE]), low(first[:TRACE]) + eye_high),
                jnp.where(flag, high(left[TRACE:]), low(first[TRACE:])),
            ],
            axis=0,
        )
        if k == 0:
            entry[1, c] = step
        else:
            old = entry[k, c]
            moved = multiply(step[:, : 2 * TRACE], old[: 2 * TRACE])
            entry[k + 1, c, : 2 * TRACE] = moved[: 2 * TRACE]
            entry[k + 1, c, 2 * TRACE :] = moved[2 * TRACE :] + old[2 * TRACE :]

    def climbing(k, c):
        left, right = ordered(k, c)
        back = to_low(left[:TRACE])
        climb[k, c, :TRACE] = back
        climb[k, c, TRACE:] = multiply(right[:TRACE, :TRACE], back) + high(right[:TRACE])

    block_row, block_lane = lax.div(row_face, FACE), lax.div(lane_face, FACE)
    face_lane = lane_face - block_lane * FACE

    def turn(e):
        within = row_face - block_row * FACE
        chosen = (block_row == block_lane) & (source_of(orient[e % cells, e // cells], within) == face_lane)
        turns[e] = chosen.astype(F32)

    def remote(source, target, send, recv, device):
        return pltpu.make_async_remote_copy(
            src_ref=source, dst_ref=target, send_sem=send, recv_sem=recv,
            device_id=device, device_id_type=pl.DeviceIdType.MESH,
        )

    sent = []
    pending = {}

    def dispatch(k, c):
        device = (partners[k], column_at)
        send, recv = send_sem.at[k, c], recv_sem.at[k, c]
        if k < rounds - 1:
            pending[k, c] = [remote(mine.at[k, c], theirs.at[k, c], send, recv, device)]
        else:
            one, two = pl.ds(0, 128), pl.ds(128, 128)
            foot = pl.ds(TRACE, 8)
            pending[k, c] = [
                remote(mine.at[k, c, :, one], theirs.at[k, c, :, one], send, recv, device),
                remote(
                    mine.at[k, c, foot, two], theirs.at[k, c, foot, two],
                    tail_sems.at[0, c], tail_sems.at[1, c], device,
                ),
            ]
        for copy in pending[k, c]:
            copy.start()
            sent.append(copy)

    sides_met = jnp.minimum(column_at, 1) + jnp.minimum(width - 1 - column_at, 1)
    ready(column_of(0), early)
    for c in range(1, cells):
        fetch(column_of(c), early)
    lift_copies[1].start()
    fetch(order, late)
    pick_copy.start()
    throughs = [passing(e) for e in column_of(0)]
    input_copies[0].wait()
    spread_jacobians(0)
    for e, through in zip(column_of(0), throughs):
        ending(e, 0, through)
    for c in range(cells):
        steps = chain(c)
        if c + 1 < cells:
            ready(column_of(c + 1), early)
            spread_jacobians(c + 1)
            throughs = []
            for e in column_of(c + 1):
                next(steps, None)
                throughs.append(passing(e))
            for e, through in zip(column_of(c + 1), throughs):
                next(steps, None)
                ending(e, 0, through)
        for _ in steps:
            pass
        if c == 0:
            pl.semaphore_wait(barrier, rounds + sides_met)
        dispatch(0, c)

    lift_copies[1].wait()
    packed[rest_at:] = pack_left(lifts[2:4].reshape(2 * TRACE, BLOCK))
    ready(order, late)
    if rounds == 1:
        for c in range(cells):
            entry[0, c] = jnp.concatenate([eye_low, eye_high, jnp.zeros((8, WIDE), F32)], axis=0)

    answering = [responses(c) for c in range(cells)]

    def rest_and_answer(e):
        for steps in answering:
            next(steps, None)
        rest(e)

    def finish_answers():
        for steps in answering:
            for _ in steps:
                pass

    tasks = []

    def later(cost, function, *values):
        tasks.append((cost, functools.partial(function, *values)))

    for index, e in enumerate(order):
        later(0.65, rest_and_answer, e)
        if index:
            later(0.2, finish, order[index - 1])
    later(0.2, finish, order[-1])
    later(0.05, finish_answers)
    for e in range(elements):
        later(0.03, turn, e)

    def work(budget):
        while tasks and (budget is None or tasks[0][0] <= budget):
            cost, task = tasks.pop(0)
            task()
            if budget is not None:
                budget -= cost

    for k in range(rounds):
        for c in range(cells):
            work(BUDGETS[c > 0])
            for copy in pending[k, c]:
                copy.wait_recv()
            if k < rounds - 1:
                left, right = ordered(k, c)
                first, node = join(left, right)
                mine[k + 1, c] = node
                dispatch(k + 1, c)
                firsts[k, c] = first
                level(k, c)
    work(None)

    top = rounds - 1
    top_flag = bits[top] == 1

    def meet(z_ours, z_other, flag):
        z_left, z_right = jnp.where(flag, z_other, z_ours), jnp.where(flag, z_ours, z_other)
        return low(z_right) + high(z_left), low(z_left) + high(z_right)

    z_ours = stack([mine[top, c, TRACE : TRACE + 1] for c in range(cells)])
    z_other = stack([theirs[top, c, TRACE : TRACE + 1] for c in range(cells)])
    met, _ = meet(z_ours, z_other, top_flag)
    turned = each(met, [below(low(theirs[top, c, :TRACE])) for c in range(cells)])
    arrived = jnp.where(top_flag, high(met), low(met + turned))
    z_in = each(arrived, [entry[top, c, : 2 * TRACE] for c in range(cells)]) + stack(
        [entry[top, c, 2 * TRACE : 2 * TRACE + 1] for c in range(cells)]
    )
    column = z_in.T
    for layer in range(layers):
        for c in range(cells):
            e = at(layer, c)
            for h in range(2):
                x[h, e : e + 1, :] = (
                    y[h, e : e + 1, :]
                    + full[e, h, 2 * TRACE : 2 * TRACE + 1]
                    + apply(column[: 2 * TRACE, c : c + 1], full[e, h, : 2 * TRACE])
                )

    pick_copy.wait()
    cross = jnp.zeros((elements, WIDE), F32)
    for h in range(2):
        x_high, x_low = split(x[h, :, :HALF])
        cross = cross + (
            jnp.dot(x_high, pick[h], preferred_element_type=F32)
            + jnp.dot(x_low, pick[h], preferred_element_type=F32)
        )
    traces[...] = cross[:, 128:]
    column = cross[:, :128].T
    for e in range(elements):
        backs[e : e + 1, :TRACE] = apply(column[:TRACE, e : e + 1], turns[e])
    up = remote(traces, got_high, cross_sems.at[0], cross_sems.at[1], (place, lax.rem(column_at + 1, width)))
    down = remote(backs, got_back, cross_sems.at[2], cross_sems.at[3], (place, lax.rem(column_at + width - 1, width)))

    @pl.when(column_at < width - 1)
    def _():
        up.start()

    @pl.when(column_at > 0)
    def _():
        down.start()

    for k in range(min(2, top)):
        for c in range(cells):
            climbing(k, c)
    for layer in range(layers):
        for c in range(cells):
            e = at(layer, c)
            if c > 0:
                from_left[e : e + 1, :] = traces[e - 1 : e, :]
            if c < cells - 1:
                from_right[e : e + 1, :] = backs[e + 1 : e + 2, :]
    firsts_at = [layer * cells for layer in range(layers)]
    lasts_at = [layer * cells + cells - 1 for layer in range(layers)]

    @pl.when(column_at > 0)
    def _():
        up.wait_recv()
        for one, two in zip(firsts_at, lasts_at):
            from_left[one : one + 1, :] = got_high[two : two + 1, :]

    @pl.when(column_at == 0)
    def _():
        for one in firsts_at:
            from_left[one : one + 1, :] = jnp.zeros((1, 128), F32)

    @pl.when(column_at < width - 1)
    def _():
        down.wait_recv()
        for one, two in zip(firsts_at, lasts_at):
            from_right[two : two + 1, :] = got_back[one : one + 1, :]

    @pl.when(column_at == width - 1)
    def _():
        for two in lasts_at:
            from_right[two : two + 1, :] = jnp.zeros((1, 128), F32)

    left_columns = from_left[...].T
    right_columns = from_right[...].T

    def loaded(e, h):
        return y[h, e : e + 1, :] - (
            apply(left_columns[:TRACE, e : e + 1], sides[e, h, :TRACE])
            + apply(right_columns[:TRACE, e : e + 1], sides[e, h, TRACE:])
        )

    for e in range(elements):
        y[0, e : e + 1, :] = loaded(e, 0)
    columns = y[0].T
    z_mine[0] = stack([
        functools.reduce(
            jnp.add,
            [apply(columns[: 2 * TRACE, at(layer, c) : at(layer, c) + 1], zmat[at(layer, c)]) for layer in range(layers)],
        )
        for c in range(cells)
    ])

    state = {}

    def gathered(layer):
        return stack([y[0, at(layer, c) : at(layer, c) + 1, :] for c in range(cells)])

    def local_sweeps():
        forward = [gathered(0)]
        for layer in range(1, layers):
            step = each(forward[-1], [below(ends[at(layer, c), 0, TRACE:]) for c in range(cells)])
            forward.append(step + gathered(layer))
        backward = jnp.zeros((8, WIDE), F32)
        for layer in reversed(range(layers)):
            before = high(forward[layer - 1]) if layer else jnp.zeros((8, WIDE), F32)
            state[layer] = backward + before
            if layer == last:
                backward = low(forward[layer])
            elif layer:
                inverse = [
                    jnp.concatenate([ends[at(layer, c), 0, :TRACE], jnp.zeros((TRACE, WIDE), F32)], axis=0)
                    for c in range(cells)
                ]
                backward = low(each(backward, inverse) + forward[layer])

    def local_rest():
        for e in range(elements):
            y[1, e : e + 1, :] = loaded(e, 1)

    def local_apply():
        for layer in range(layers):
            column = state[layer].T
            for c in range(cells):
                e = at(layer, c)
                for h in range(2):
                    x[h, e : e + 1, :] = y[h, e : e + 1, :] + apply(column[: 2 * TRACE, c : c + 1], ends[e, h])

    for task in (local_sweeps, local_rest, local_apply):
        later(0, task)
    z_in = jnp.zeros((8, WIDE), F32)
    for k in range(rounds):
        flag = bits[k] == 1
        copy = remote(z_mine.at[k], z_theirs.at[k], z_send.at[k], z_recv.at[k], (partners[k], column_at))
        copy.start()
        sent.append(copy)
        for c in range(cells):
            reach_level(k, c)
            if 2 <= k + 1 < top:
                climbing(k + 1, c)
        if k < rounds - 1:
            if tasks:
                tasks.pop(0)[1]()
        else:
            work(None)
        copy.wait_recv()
        met, kept = meet(z_mine[k], z_theirs[k], flag)
        if k < rounds - 1:
            z_mine[k + 1] = each(met, [climb[k, c] for c in range(cells)]) + kept
        z_in = z_in + each(met, [reach[k, c] for c in range(cells)])

    column = z_in.T
    for layer in range(layers):
        for c in range(cells):
            e = at(layer, c)
            for h in range(2):
                x[h, e : e + 1, :] = x[h, e : e + 1, :] + apply(
                    column[: 2 * TRACE, c : c + 1], full[e, h, : 2 * TRACE]
                )
    for slot, i in enumerate(SLOTS):
        for v in range(VARS):
            target = (v * EXTENT + i) * FACE
            source = (slot % 2) * TRACE + v * FACE
            natural[:, target : target + FACE] = x[slot // 2, :, source : source + FACE]
    for layer in range(layers):
        out[layer] = natural[layer * cells : (layer + 1) * cells, :]

    for copy in sent:
        copy.wait_send()

    @pl.when(column_at < width - 1)
    def _():
        up.wait_send()

    @pl.when(column_at > 0)
    def _():
        down.wait_send()


def picker():
    table = np.zeros((2, HALF, WIDE), np.float32)
    for slot, i in enumerate(SLOTS):
        for v in range(VARS):
            for k in range(EXTENT):
                source = (slot % 2) * TRACE + v * FACE + k
                target = v * FACE + i * EXTENT + k
                table[slot // 2, source, target] = 1.0
                table[slot // 2, source + (EXTENT - 1) * EXTENT, 128 + target] = 1.0
    return table


def on_device(width, count, vector, inverses, lift_maps, jacobians, orient):
    layers, cells = vector.shape[:2]
    elements = layers * cells
    rounds = count.bit_length() - 1
    inv = inverses.reshape(elements, VARS, EXTENT, FACE, BLOCK)
    flat = jacobians.transpose(0, 1, 3, 4, 2, 5).reshape(elements, VARS, VARS, 4, FACE)
    pick = jnp.asarray(picker(), BF16)
    vec_rows = -(-elements // 16) * 16
    depth = 4 * TRACE + vec_rows
    vmem = pl.BlockSpec(memory_space=pltpu.VMEM)
    hbm = pl.BlockSpec(memory_space=pltpu.HBM)
    tall = 2 * TRACE + 8
    result = pl.pallas_call(
        functools.partial(kernel, layers, cells, width, rounds),
        out_shape=jax.ShapeDtypeStruct((layers, cells, BLOCK), F32),
        in_specs=[hbm, hbm, hbm, hbm, pl.BlockSpec(memory_space=pltpu.SMEM), hbm],
        out_specs=vmem,
        scratch_shapes=[
            pltpu.VMEM((elements, EXTENT, VARS, FACE, BLOCK), F32),
            pltpu.SemaphoreType.DMA((elements, EXTENT)),
            pltpu.VMEM((4, TRACE, BLOCK), F32),
            pltpu.SemaphoreType.DMA((2,)),
            pltpu.VMEM((2, HALF, WIDE), BF16),
            pltpu.SemaphoreType.DMA((1,)),
            pltpu.VMEM((layers, cells, BLOCK), F32),
            pltpu.VMEM((elements, VARS, VARS, 4, FACE), F32),
            pltpu.SemaphoreType.DMA((2,)),
            pltpu.VMEM((vec_rows, BLOCK), F32),
            pltpu.VMEM((elements, VARS, 8, WIDE), F32),
            pltpu.VMEM((depth, 4 * WIDE), BF16),
            pltpu.VMEM((elements, HALF, 4 * WIDE), BF16),
            pltpu.VMEM((elements, 2, 2 * TRACE, WIDE), F32),
            pltpu.VMEM((elements, 2, 2 * TRACE, WIDE), F32),
            pltpu.VMEM((elements, tall, WIDE), F32),
            pltpu.VMEM((elements, 2, tall, WIDE), F32),
            pltpu.VMEM((2, elements, WIDE), F32),
            pltpu.VMEM((2, elements, WIDE), F32),
            pltpu.VMEM((rounds, cells, tall, WIDE), F32),
            pltpu.VMEM((rounds, cells, 2 * TRACE, WIDE), F32),
            pltpu.VMEM((rounds, cells, 2 * TRACE, WIDE), F32),
            pltpu.VMEM((elements, 2 * TRACE, WIDE), F32),
            pltpu.VMEM((rounds, cells, ROWS, WIDE), F32),
            pltpu.VMEM((rounds, cells, ROWS, WIDE), F32),
            pltpu.VMEM((rounds, cells, ROWS, WIDE), F32),
            pltpu.SemaphoreType.DMA((rounds, cells)),
            pltpu.SemaphoreType.DMA((rounds, cells)),
            pltpu.SemaphoreType.DMA((2, cells)),
            pltpu.VMEM((rounds, 8, WIDE), F32),
            pltpu.VMEM((rounds, 8, WIDE), F32),
            pltpu.SemaphoreType.DMA((rounds,)),
            pltpu.SemaphoreType.DMA((rounds,)),
            pltpu.VMEM((elements, TRACE, TRACE), F32),
            pltpu.VMEM((elements, 128), F32),
            pltpu.VMEM((elements, 128), F32),
            pltpu.VMEM((elements, 128), F32),
            pltpu.VMEM((elements, 128), F32),
            pltpu.VMEM((elements, 128), F32),
            pltpu.VMEM((elements, 128), F32),
            pltpu.SemaphoreType.DMA((4,)),
            pltpu.VMEM((elements, BLOCK), F32),
        ],
        compiler_params=pltpu.CompilerParams(
            collective_id=0, has_side_effects=True, vmem_limit_bytes=62 * 1024 * 1024
        ),
    )(inv, vector, lift_maps.transpose(0, 2, 1), flat, orient.T, pick)
    return result


def solution(mesh):
    in_specs = (
        P("stream", "cross", None),
        P("stream", "cross", None, None),
        P(),
        P("stream", "cross", None, None, None, None),
        P("stream", "cross"),
    )
    out_specs = P("stream", "cross", None)
    return jax.shard_map(
        functools.partial(on_device, mesh.shape["cross"], mesh.shape["stream"]),
        mesh=mesh, in_specs=in_specs, out_specs=out_specs, check_vma=False,
    )
```

```python
import functools

import jax
import jax.numpy as jnp
import numpy as np
from jax import lax
from jax.experimental import pallas as pl
from jax.experimental.pallas import tpu as pltpu
from jax.sharding import PartitionSpec as P

ORDER = 3
EXTENT = ORDER + 1
VARS = 5
FACE = EXTENT * EXTENT
TRACE = VARS * FACE
BLOCK = VARS * FACE * EXTENT
HALF = BLOCK // 2
SLOTS = (0, EXTENT - 1) + tuple(range(1, EXTENT - 1))
WIDE = 256
ROWS = TRACE + 8
BUDGETS = (1.4, 0.7)
F32 = jnp.float32
BF16 = jnp.bfloat16


def split(value):
    high = value.astype(BF16)
    return high, (value - high.astype(F32)).astype(BF16)


def product(left, right, transposed=False):
    dims = (((1,), (1 if transposed else 0,)), ((), ()))
    dot = functools.partial(lax.dot_general, dimension_numbers=dims, preferred_element_type=F32)
    left_high, left_low = left
    right_high, right_low = right
    return dot(left_high, right_high) + (dot(left_high, right_low) + dot(left_low, right_high))


def spread(value):
    wide = BLOCK - BLOCK % WIDE
    high_part, low_part = split(value)
    none = jnp.zeros((value.shape[0], WIDE - 3 * (BLOCK - wide)), BF16)
    return (high_part[:, :wide], low_part[:, :wide]), (high_part[:, wide:], low_part[:, wide:]), none


def pack_left(value):
    (body_high, body_low), (tail_high, tail_low), none = spread(value)
    return jnp.concatenate([body_high, body_high, body_low, tail_high, tail_high, tail_low, none], axis=1)


def pack_right(value):
    (body_high, body_low), (tail_high, tail_low), none = spread(value)
    return jnp.concatenate([body_high, body_low, body_high, tail_high, tail_low, tail_high, none], axis=1)


def against(left, right):
    return lax.dot_general(left, right, (((1,), (1,)), ((), ())), preferred_element_type=F32)


def faced(face, value):
    high_part, low_part = split(value)
    return jnp.dot(
        face, jnp.concatenate([high_part, low_part, high_part], axis=0), preferred_element_type=F32
    )


def multiply(left, right):
    return product(split(left), split(right))


def lanes(shape):
    return lax.broadcasted_iota(jnp.int32, shape, 1)


def rows(shape):
    return lax.broadcasted_iota(jnp.int32, shape, 0)


def keep(mask, value):
    return jnp.where(mask, value, 0.0)


def low(value):
    return keep(lanes(value.shape) < TRACE, value)


def high(value):
    lane = lanes(value.shape)
    return keep((lane >= TRACE) & (lane < 2 * TRACE), value)


def below(value):
    return jnp.concatenate([jnp.zeros((TRACE, value.shape[1]), F32), value], axis=0)


def to_low(value):
    return low(pltpu.roll(value, WIDE - 2 * TRACE, 1))


def join(left, right):
    lane = lanes((TRACE, WIDE))
    through = below(keep(lane < 2 * TRACE, right[:TRACE]))
    first = multiply(left[:, : 2 * TRACE], through)
    lane_all = lanes((ROWS, WIDE))
    row_all = rows((ROWS, WIDE))
    first = first + keep((lane_all >= 2 * TRACE) | (row_all >= TRACE), right)
    back = left[:TRACE]
    through = jnp.concatenate(
        [to_low(back), jnp.zeros((TRACE, WIDE), F32), keep(lane >= 2 * TRACE, back)], axis=0
    )
    second = multiply(first[:, : 3 * TRACE], through)
    middle = (lane_all >= TRACE) & (lane_all < 2 * TRACE)
    return first, second + keep(middle, first) + keep(lane_all < TRACE, left)


def apply(column, matrix):
    return jnp.sum(column * matrix, axis=0, keepdims=True)


def stack(parts):
    total = jnp.zeros((8, parts[0].shape[1]), F32)
    row = rows(total.shape)
    for index, part in enumerate(parts):
        total = jnp.where(row == index, jnp.broadcast_to(part, total.shape), total)
    return total


def each(z, matrices):
    pieces = split(z[:, : 2 * TRACE])
    row = rows((8, WIDE))
    total = jnp.zeros((8, WIDE), F32)
    for index, matrix in enumerate(matrices):
        total = jnp.where(row == index, product(pieces, split(matrix)), total)
    return total


def kernel(
    layers, cells, width, rounds,
    inv, vector_source, lift_maps, jacobian_source, orient_source, pick_source, out,
    blocks, block_sem, lifts, lift_sem, pick, pick_sem, vector, jacobians, orient, input_sem, vecs, jac_rows, packed, near,
    ends, sides, inner, full, y, x, entry, climb, climb_got, climb_send, climb_recv, reach, zmat, firsts,
    mine, theirs, send_sem, recv_sem, tail_sems, z_mine, z_theirs, z_send, z_recv,
    turns, traces, backs, got_high, got_back, from_left, from_right, cross_sems, natural,
):
    elements = layers * cells
    place = lax.axis_index("stream")
    column_at = lax.axis_index("cross")
    last = layers - 1
    vec_rows = vecs.shape[0]

    def at(layer, c):
        return layer * cells + c

    order = [at(layer, c) for c in range(cells) for layer in range(layers)]

    lift_copies = [
        pltpu.make_async_copy(lift_maps.at[2 * h : 2 * h + 2], lifts.at[2 * h : 2 * h + 2], lift_sem.at[h])
        for h in range(2)
    ]

    def block_copies(e, slots):
        return [
            pltpu.make_async_copy(inv.at[e, :, SLOTS[s]], blocks.at[e, s], block_sem.at[e, s]) for s in slots
        ]

    early, late = (0, 1), tuple(range(2, EXTENT))
    def column_of(c):
        return [at(layer, c) for layer in range(layers)]

    def fetch(members, slots):
        for e in members:
            for copy in block_copies(e, slots):
                copy.start()

    def ready(members, slots):
        for e in members:
            for copy in block_copies(e, slots):
                copy.wait()

    input_copies = [
        pltpu.make_async_copy(jacobian_source, jacobians, input_sem.at[0]),
        pltpu.make_async_copy(vector_source, vector, input_sem.at[1]),
        pltpu.make_async_copy(orient_source, orient, input_sem.at[2]),
    ]
    input_copies[1].start()
    lift_copies[0].start()
    fetch(column_of(0), early)
    input_copies[0].start()
    input_copies[2].start()
    pick_copy = pltpu.make_async_copy(pick_source, pick, pick_sem.at[0])

    bits = [lax.rem(place // (1 << k), 2) for k in range(rounds)]
    partners = [place + (1 - 2 * bits[k]) * (1 << k) for k in range(rounds)]
    paired = min(2, rounds)
    groups = [tuple(range(paired))] + [(k,) for k in range(paired, rounds)]
    friends = []
    for group in groups:
        near_one, far_one = partners[group[0]], partners[group[-1]]
        friends.append([near_one, far_one, near_one + far_one - place] if len(group) == 2 else [near_one])
    met_count = sum(len(friend) for friend in friends)
    barrier = pltpu.get_barrier_semaphore()
    for friend in friends:
        for partner in friend:
            pl.semaphore_signal(barrier, inc=1, device_id=(partner, column_at), device_id_type=pl.DeviceIdType.MESH)

    @pl.when(column_at > 0)
    def _():
        pl.semaphore_signal(barrier, inc=1, device_id=(place, column_at - 1), device_id_type=pl.DeviceIdType.MESH)

    @pl.when(column_at < width - 1)
    def _():
        pl.semaphore_signal(barrier, inc=1, device_id=(place, column_at + 1), device_id_type=pl.DeviceIdType.MESH)

    vecs[...] = jnp.zeros_like(vecs)
    jac_rows[...] = jnp.zeros_like(jac_rows)
    backs[...] = jnp.zeros_like(backs)

    def spread_jacobians(c):
        for e in column_of(c):
            for v in range(VARS):
                for w in range(VARS):
                    jac_rows[e, w, :4, v * FACE : (v + 1) * FACE] = jacobians[e, v, w]
            for w in range(VARS):
                value = jac_rows[e, w]
                jac_rows[e, w] = value + pltpu.roll(value, TRACE, 1) + pltpu.roll(value, 2 * TRACE, 1)

    input_copies[1].wait()
    for e in range(elements):
        vecs[e : e + 1, :] = vector[e // cells, e % cells : e % cells + 1, :]

    row_face = rows((TRACE, TRACE))
    lane_face = lanes((TRACE, TRACE))
    row_wide = lax.rem(rows((TRACE, WIDE)), FACE)
    lane_wide = lax.rem(lanes((TRACE, WIDE)), FACE)
    same = row_wide == lane_wide
    leading = lanes((TRACE, WIDE)) < 2 * TRACE
    lane_line = lax.rem(lanes((1, WIDE)), FACE)
    eye = rows((TRACE, WIDE)) == lanes((TRACE, WIDE))
    eye_low = eye.astype(F32)
    eye_high = (rows((TRACE, WIDE)) + TRACE == lanes((TRACE, WIDE))).astype(F32)
    first_row = rows((8, WIDE)) == 0

    def source_of(code, node_index):
        first = lax.div(node_index, EXTENT)
        second = node_index - first * EXTENT
        first, second = (
            first + lax.rem(code, 2) * (second - first),
            second + lax.rem(code, 2) * (first - second),
        )
        first = first + lax.rem(code // 2, 2) * (EXTENT - 1 - 2 * first)
        second = second + lax.rem(code // 4, 2) * (EXTENT - 1 - 2 * second)
        return first * EXTENT + second

    def face(e, m, chosen):
        tall = jnp.concatenate(
            [jnp.broadcast_to(jac_rows[e, w, m : m + 1, :], (FACE, WIDE)) for w in range(VARS)],
            axis=0,
        )
        value = keep(chosen, tall)
        value = jnp.where(leading, value, value - value.astype(BF16).astype(F32))
        return value[:, : 3 * TRACE].astype(BF16)

    def half(e, h):
        return pack_right(blocks[e, 2 * h : 2 * h + 2].reshape(HALF, BLOCK))

    def ending(e, h, through):
        ends[e, h, TRACE:, :HALF] = -faced(face(e, 0, same), through[:TRACE])
        ends[e, h, :TRACE, :HALF] = -faced(face(e, 1, same), through[TRACE : 2 * TRACE])

    vec_at, rest_at = 2 * TRACE, 2 * TRACE + vec_rows
    packed[vec_at:rest_at] = pack_left(vecs[...])
    lift_copies[0].wait()
    packed[:vec_at] = pack_left(lifts[0:2].reshape(2 * TRACE, BLOCK))

    def passing(e):
        block = half(e, 0)
        near[e] = block
        through = against(packed[:rest_at], block)
        y[0, e : e + 1, :HALF] = through[vec_at + e : vec_at + e + 1]
        return through

    held = {}

    def rest_pass(e):
        held[e] = against(packed[...], half(e, 1)), against(packed[rest_at:], near[e])

    def rest_end(e):
        through, beside = held.pop(e)
        y[1, e : e + 1, :HALF] = through[vec_at + e : vec_at + e + 1]
        ending(e, 1, through)
        chosen = row_wide == source_of(orient[e % cells, e // cells], lane_line)
        faces = face(e, 2, chosen), face(e, 3, same)
        for h, value in enumerate((beside, through[rest_at:])):
            for m in range(2):
                sides[e, h, m * TRACE : (m + 1) * TRACE, :HALF] = faced(
                    faces[m], value[m * TRACE : (m + 1) * TRACE]
                )

    def finish(e):
        for h in range(2):
            full[e, h] = product(split(inner[e, :, : 2 * TRACE]), split(ends[e, h]))

    def chain(c):
        up = [ends[at(layer, c), 0, TRACE:] for layer in range(layers)]
        down = [ends[at(layer, c), 0, :TRACE] for layer in range(layers)]

        def bottom(layer):
            e = at(layer, c)
            return keep(first_row, jnp.broadcast_to(y[0, e : e + 1, :], (8, WIDE)))

        forward = [jnp.concatenate([up[0], bottom(0)], axis=0)]
        for layer in range(1, layers):
            step = multiply(forward[-1][:, : 2 * TRACE], below(up[layer]))
            forward.append(step + below(bottom(layer)))
            yield
        none = jnp.zeros((ROWS, WIDE), F32)
        backward = jnp.concatenate([eye_low, none], axis=0)
        for layer in reversed(range(layers)):
            before = forward[layer - 1] if layer else jnp.concatenate([eye_high, none[TRACE:]], axis=0)
            inner[at(layer, c)] = backward + below(high(before))
            if layer == last:
                backward = low(jnp.concatenate([down[layer], forward[layer]], axis=0))
            else:
                backward = low(multiply(backward[:, :TRACE], down[layer]) + below(forward[layer]))
                yield
        whole = backward[TRACE:] + high(forward[last])
        extra = pltpu.roll(backward[:TRACE], 2 * TRACE, 1)
        mine[0, c, TRACE:] = whole[TRACE:]
        mine[0, c, :TRACE] = whole[:TRACE] + extra

    def responses(c):
        behind = eye_low
        reach_low, after = [], []
        for layer in range(layers):
            reach_low.append(behind)
            e = at(layer, c)
            pair = jnp.concatenate([ends[e, 0, TRACE:], ends[e, 0, :TRACE]], axis=0)
            if layer == 0:
                both = low(pair)
            else:
                both = low(multiply(pair[:, :TRACE], behind))
                yield
            after.append(both[:TRACE])
            behind = both[TRACE:]
        ahead = eye_high
        for layer in reversed(range(layers)):
            e = at(layer, c)
            zmat[e, :TRACE] = reach_low[layer]
            zmat[e, TRACE:] = ahead
            if layer:
                if layer == last:
                    ahead = high(ends[e, 0, TRACE:]) + after[layer]
                else:
                    ahead = multiply(ends[e, 0, TRACE:, : 2 * TRACE], below(ahead)) + after[layer]
                    yield

    def ordered(k, c):
        flag = bits[k] == 1
        ours, other = mine[k, c], theirs[k, c]
        return jnp.where(flag, other, ours), jnp.where(flag, ours, other)

    def reaching(k, c, first):
        flag = bits[k] == 1
        if k == 0:
            near, far = eye_low, low(first)
            ahead = eye_high
        else:
            near, ahead = entry[k, c, :TRACE], entry[k, c, TRACE : 2 * TRACE]
            far = multiply(first[:, :TRACE], near)
        reach[k, c, :TRACE] = jnp.where(flag, 0.0, near)
        reach[k, c, TRACE:] = jnp.where(flag, ahead, far)

    def reach_level(k, c):
        other = jnp.where(bits[k] == 1, mine[k, c, :TRACE, :128], theirs[k, c, :TRACE, :128])
        reaching(k, c, jnp.concatenate([other, jnp.zeros((TRACE, WIDE - 128), F32)], axis=1))

    def level(k, c):
        left, right = ordered(k, c)
        flag = bits[k] == 1
        first = firsts[k, c]
        step = jnp.concatenate(
            [
                jnp.where(flag, eye_low, to_low(right[:TRACE])),
                jnp.where(flag, high(left[:TRACE]), low(first[:TRACE]) + eye_high),
                jnp.where(flag, high(left[TRACE:]), low(first[TRACE:])),
            ],
            axis=0,
        )
        if k == 0:
            entry[1, c] = step
        else:
            old = entry[k, c]
            moved = multiply(step[:, : 2 * TRACE], old[: 2 * TRACE])
            entry[k + 1, c, : 2 * TRACE] = moved[: 2 * TRACE]
            entry[k + 1, c, 2 * TRACE :] = moved[2 * TRACE :] + old[2 * TRACE :]

    def climbing(k, c):
        left, right = ordered(k, c)
        back = left[:TRACE]
        turned = low(multiply(right[:TRACE, :TRACE], to_low(back)))
        climb[k, c] = turned + high(right[:TRACE]) + keep(lanes((TRACE, WIDE)) >= 2 * TRACE, back)

    def climber(packed_climb):
        return jnp.concatenate([to_low(packed_climb), packed_climb], axis=0)

    alike = lax.div(row_face, FACE) == lax.div(lane_face, FACE)
    small_row = rows((FACE, TRACE))
    small_lane = lax.rem(lanes((FACE, TRACE)), FACE)

    def turn(e):
        chosen = (source_of(orient[e % cells, e // cells], small_row) == small_lane).astype(F32)
        turns[e] = keep(alike, jnp.concatenate([chosen] * VARS, axis=0))

    def remote(source, target, send, recv, device):
        return pltpu.make_async_remote_copy(
            src_ref=source, dst_ref=target, send_sem=send, recv_sem=recv,
            device_id=device, device_id_type=pl.DeviceIdType.MESH,
        )

    sent = []
    pending = {}
    climb_copies = {}

    def dispatch(k, c):
        device = (partners[k], column_at)
        send, recv = send_sem.at[k, c], recv_sem.at[k, c]
        if k < rounds - 1:
            pending[k, c] = [remote(mine.at[k, c], theirs.at[k, c], send, recv, device)]
        else:
            one, two = pl.ds(0, 128), pl.ds(128, 128)
            foot = pl.ds(TRACE, 8)
            pending[k, c] = [
                remote(mine.at[k, c, :, one], theirs.at[k, c, :, one], send, recv, device),
                remote(
                    mine.at[k, c, foot, two], theirs.at[k, c, foot, two],
                    tail_sems.at[0, c], tail_sems.at[1, c], device,
                ),
            ]
        for copy in pending[k, c]:
            copy.start()
            sent.append(copy)

    sides_met = jnp.minimum(column_at, 1) + jnp.minimum(width - 1 - column_at, 1)
    ready(column_of(0), early)
    for c in range(1, cells):
        fetch(column_of(c), early)
    lift_copies[1].start()
    fetch(order, late)
    pick_copy.start()
    throughs = [passing(e) for e in column_of(0)]
    input_copies[0].wait()
    spread_jacobians(0)
    for e, through in zip(column_of(0), throughs):
        ending(e, 0, through)
    for c in range(cells):
        steps = chain(c)
        if c + 1 < cells:
            ready(column_of(c + 1), early)
            spread_jacobians(c + 1)
            throughs = []
            for e in column_of(c + 1):
                next(steps, None)
                throughs.append(passing(e))
            for e, through in zip(column_of(c + 1), throughs):
                next(steps, None)
                ending(e, 0, through)
        for _ in steps:
            pass
        if c == 0:
            pl.semaphore_wait(barrier, met_count + sides_met)
        dispatch(0, c)

    lift_copies[1].wait()
    input_copies[2].wait()
    packed[rest_at:] = pack_left(lifts[2:4].reshape(2 * TRACE, BLOCK))
    ready(order, late)
    if rounds == 1:
        for c in range(cells):
            entry[0, c] = jnp.concatenate([eye_low, eye_high, jnp.zeros((8, WIDE), F32)], axis=0)

    answering = [responses(c) for c in range(cells)]

    def stage(index):
        if index < elements:
            rest_pass(order[index])
        if 0 < index <= elements:
            rest_end(order[index - 1])
        if index > 1:
            finish(order[index - 2])
        for steps in answering:
            next(steps, None)

    def finish_answers():
        for steps in answering:
            for _ in steps:
                pass

    tasks = []

    def later(cost, function, *values):
        tasks.append((cost, functools.partial(function, *values)))

    for index in range(elements + 2):
        later(0.65, stage, index)
    later(0.05, finish_answers)
    for e in range(elements):
        later(0.03, turn, e)

    def work(budget):
        while tasks and (budget is None or tasks[0][0] <= budget):
            cost, task = tasks.pop(0)
            task()
            if budget is not None:
                budget -= cost

    for k in range(rounds):
        for c in range(cells):
            work(BUDGETS[c > 0])
            for copy in pending[k, c]:
                copy.wait_recv()
            if k < rounds - 1:
                left, right = ordered(k, c)
                first, node = join(left, right)
                mine[k + 1, c] = node
                dispatch(k + 1, c)
                firsts[k, c] = first
                level(k, c)
                if k == 0 and c == cells - 1:
                    for other in range(cells):
                        climbing(k, other)
                        copy = remote(
                            climb.at[k, other], climb_got.at[k, other],
                            climb_send.at[k, other], climb_recv.at[k, other], (partners[k + 1], column_at),
                        )
                        copy.start()
                        sent.append(copy)
                        climb_copies[k, other] = copy
    work(None)

    top = rounds - 1
    top_flag = bits[top] == 1

    def meet(z_ours, z_other, flag):
        z_left, z_right = jnp.where(flag, z_other, z_ours), jnp.where(flag, z_ours, z_other)
        return low(z_right) + high(z_left), low(z_left) + high(z_right)

    z_ours = stack([mine[top, c, TRACE : TRACE + 1] for c in range(cells)])
    z_other = stack([theirs[top, c, TRACE : TRACE + 1] for c in range(cells)])
    met, _ = meet(z_ours, z_other, top_flag)
    turned = each(met, [below(low(theirs[top, c, :TRACE])) for c in range(cells)])
    arrived = jnp.where(top_flag, high(met), low(met + turned))
    z_in = each(arrived, [entry[top, c, : 2 * TRACE] for c in range(cells)]) + stack(
        [entry[top, c, 2 * TRACE : 2 * TRACE + 1] for c in range(cells)]
    )
    column = z_in.T
    for layer in range(layers):
        for c in range(cells):
            e = at(layer, c)
            for h in range(2):
                x[h, e : e + 1, :] = (
                    y[h, e : e + 1, :]
                    + full[e, h, 2 * TRACE : 2 * TRACE + 1]
                    + apply(column[: 2 * TRACE, c : c + 1], full[e, h, : 2 * TRACE])
                )

    pick_copy.wait()
    cross = jnp.zeros((elements, WIDE), F32)
    for h in range(2):
        x_high, x_low = split(x[h, :, :HALF])
        cross = cross + (
            jnp.dot(x_high, pick[h], preferred_element_type=F32)
            + jnp.dot(x_low, pick[h], preferred_element_type=F32)
        )
    traces[...] = cross[:, 128:]
    column = cross[:, :128].T
    for e in range(elements):
        backs[e : e + 1, :TRACE] = apply(column[:TRACE, e : e + 1], turns[e])
    up = remote(traces, got_high, cross_sems.at[0], cross_sems.at[1], (place, lax.rem(column_at + 1, width)))
    down = remote(backs, got_back, cross_sems.at[2], cross_sems.at[3], (place, lax.rem(column_at + width - 1, width)))

    @pl.when(column_at < width - 1)
    def _():
        up.start()

    @pl.when(column_at > 0)
    def _():
        down.start()

    def prepare(g):
        for k in groups[g]:
            for c in range(cells):
                reach_level(k, c)
                if 0 < k < top:
                    climbing(k, c)

    prepare(0)
    for layer in range(layers):
        for c in range(cells):
            e = at(layer, c)
            if c > 0:
                from_left[e : e + 1, :] = traces[e - 1 : e, :]
            if c < cells - 1:
                from_right[e : e + 1, :] = backs[e + 1 : e + 2, :]
    firsts_at = [layer * cells for layer in range(layers)]
    lasts_at = [layer * cells + cells - 1 for layer in range(layers)]

    @pl.when(column_at > 0)
    def _():
        up.wait_recv()
        for one, two in zip(firsts_at, lasts_at):
            from_left[one : one + 1, :] = got_high[two : two + 1, :]

    @pl.when(column_at == 0)
    def _():
        for one in firsts_at:
            from_left[one : one + 1, :] = jnp.zeros((1, 128), F32)

    @pl.when(column_at < width - 1)
    def _():
        down.wait_recv()
        for one, two in zip(firsts_at, lasts_at):
            from_right[two : two + 1, :] = got_back[one : one + 1, :]

    @pl.when(column_at == width - 1)
    def _():
        for two in lasts_at:
            from_right[two : two + 1, :] = jnp.zeros((1, 128), F32)

    left_columns = from_left[...].T
    right_columns = from_right[...].T

    def loaded(e, h):
        return y[h, e : e + 1, :] - (
            apply(left_columns[:TRACE, e : e + 1], sides[e, h, :TRACE])
            + apply(right_columns[:TRACE, e : e + 1], sides[e, h, TRACE:])
        )

    for e in range(elements):
        y[0, e : e + 1, :] = loaded(e, 0)
    columns = y[0].T
    z_mine[0] = stack([
        functools.reduce(
            jnp.add,
            [apply(columns[: 2 * TRACE, at(layer, c) : at(layer, c) + 1], zmat[at(layer, c)]) for layer in range(layers)],
        )
        for c in range(cells)
    ])

    state = {}

    def gathered(layer):
        return stack([y[0, at(layer, c) : at(layer, c) + 1, :] for c in range(cells)])

    def local_sweeps():
        forward = [gathered(0)]
        for layer in range(1, layers):
            step = each(forward[-1], [below(ends[at(layer, c), 0, TRACE:]) for c in range(cells)])
            forward.append(step + gathered(layer))
        backward = jnp.zeros((8, WIDE), F32)
        for layer in reversed(range(layers)):
            before = high(forward[layer - 1]) if layer else jnp.zeros((8, WIDE), F32)
            state[layer] = backward + before
            if layer == last:
                backward = low(forward[layer])
            elif layer:
                inverse = [
                    jnp.concatenate([ends[at(layer, c), 0, :TRACE], jnp.zeros((TRACE, WIDE), F32)], axis=0)
                    for c in range(cells)
                ]
                backward = low(each(backward, inverse) + forward[layer])

    def local_rest():
        for e in range(elements):
            y[1, e : e + 1, :] = loaded(e, 1)

    def local_settle():
        local_rest()
        for layer in range(layers):
            column = state[layer].T
            for c in range(cells):
                e = at(layer, c)
                for h in range(2):
                    x[h, e : e + 1, :] = y[h, e : e + 1, :] + apply(column[: 2 * TRACE, c : c + 1], ends[e, h])

    for task in (local_sweeps, local_settle):
        later(0, task)
    z_in = jnp.zeros((8, WIDE), F32)
    for g, group in enumerate(groups):
        copies = [
            remote(z_mine.at[g], z_theirs.at[g, i], z_send.at[g, i], z_recv.at[g, i], (partner, column_at))
            for i, partner in enumerate(friends[g])
        ]
        for copy in copies:
            copy.start()
            sent.append(copy)
        if g + 1 < len(groups):
            prepare(g + 1)
            tasks.pop(0)[1]() if tasks else None
        else:
            work(None)
        k = group[0]
        if len(group) == 2:
            for c in range(cells):
                climb_copies[k, c].wait_recv()
        for copy in copies:
            copy.wait_recv()
        flag = bits[k] == 1
        met, kept = meet(z_mine[g], z_theirs[g, 0], flag)
        z_in = z_in + each(met, [reach[k, c] for c in range(cells)])
        if len(group) == 2:
            both, stays = meet(z_theirs[g, 1], z_theirs[g, 2], flag)
            ours = kept + each(met, [climber(climb[k, c]) for c in range(cells)])
            other = stays + each(both, [climber(climb_got[k, c]) for c in range(cells)])
            k = group[1]
            met, kept = meet(ours, other, bits[k] == 1)
            z_in = z_in + each(met, [reach[k, c] for c in range(cells)])
        if k < top:
            z_mine[g + 1] = kept + each(met, [climber(climb[k, c]) for c in range(cells)])

    column = z_in.T
    for layer in range(layers):
        for c in range(cells):
            e = at(layer, c)
            for h in range(2):
                x[h, e : e + 1, :] = x[h, e : e + 1, :] + apply(
                    column[: 2 * TRACE, c : c + 1], full[e, h, : 2 * TRACE]
                )
    for slot, i in enumerate(SLOTS):
        for v in range(VARS):
            target = (v * EXTENT + i) * FACE
            source = (slot % 2) * TRACE + v * FACE
            natural[:, target : target + FACE] = x[slot // 2, :, source : source + FACE]
    for layer in range(layers):
        out[layer] = natural[layer * cells : (layer + 1) * cells, :]

    for copy in sent:
        copy.wait_send()

    @pl.when(column_at < width - 1)
    def _():
        up.wait_send()

    @pl.when(column_at > 0)
    def _():
        down.wait_send()


def picker():
    table = np.zeros((2, HALF, WIDE), np.float32)
    for slot, i in enumerate(SLOTS):
        for v in range(VARS):
            for k in range(EXTENT):
                source = (slot % 2) * TRACE + v * FACE + k
                target = v * FACE + i * EXTENT + k
                table[slot // 2, source, target] = 1.0
                table[slot // 2, source + (EXTENT - 1) * EXTENT, 128 + target] = 1.0
    return table


def on_device(width, count, vector, inverses, lift_maps, jacobians, orient):
    layers, cells = vector.shape[:2]
    elements = layers * cells
    rounds = count.bit_length() - 1
    inv = inverses.reshape(elements, VARS, EXTENT, FACE, BLOCK)
    flat = jacobians.transpose(0, 1, 3, 4, 2, 5).reshape(elements, VARS, VARS, 4, FACE)
    pick = jnp.asarray(picker(), BF16)
    vec_rows = -(-elements // 16) * 16
    depth = 4 * TRACE + vec_rows
    vmem = pl.BlockSpec(memory_space=pltpu.VMEM)
    hbm = pl.BlockSpec(memory_space=pltpu.HBM)
    tall = 2 * TRACE + 8
    groups = max(1, rounds - 1)
    result = pl.pallas_call(
        functools.partial(kernel, layers, cells, width, rounds),
        out_shape=pltpu.VMEM((layers, cells, BLOCK), F32),
        in_specs=[hbm] * 6,
        out_specs=vmem,
        scratch_shapes=[
            pltpu.VMEM((elements, EXTENT, VARS, FACE, BLOCK), F32),
            pltpu.SemaphoreType.DMA((elements, EXTENT)),
            pltpu.VMEM((4, TRACE, BLOCK), F32),
            pltpu.SemaphoreType.DMA((2,)),
            pltpu.VMEM((2, HALF, WIDE), BF16),
            pltpu.SemaphoreType.DMA((1,)),
            pltpu.VMEM((layers, cells, BLOCK), F32),
            pltpu.VMEM((elements, VARS, VARS, 4, FACE), F32),
            pltpu.SMEM((cells, layers), jnp.int32),
            pltpu.SemaphoreType.DMA((3,)),
            pltpu.VMEM((vec_rows, BLOCK), F32),
            pltpu.VMEM((elements, VARS, 8, WIDE), F32),
            pltpu.VMEM((depth, 4 * WIDE), BF16),
            pltpu.VMEM((elements, HALF, 4 * WIDE), BF16),
            pltpu.VMEM((elements, 2, 2 * TRACE, WIDE), F32),
            pltpu.VMEM((elements, 2, 2 * TRACE, WIDE), F32),
            pltpu.VMEM((elements, tall, WIDE), F32),
            pltpu.VMEM((elements, 2, tall, WIDE), F32),
            pltpu.VMEM((2, elements, WIDE), F32),
            pltpu.VMEM((2, elements, WIDE), F32),
            pltpu.VMEM((rounds, cells, tall, WIDE), F32),
            pltpu.VMEM((rounds, cells, TRACE, WIDE), F32),
            pltpu.VMEM((rounds, cells, TRACE, WIDE), F32),
            pltpu.SemaphoreType.DMA((rounds, cells)),
            pltpu.SemaphoreType.DMA((rounds, cells)),
            pltpu.VMEM((rounds, cells, 2 * TRACE, WIDE), F32),
            pltpu.VMEM((elements, 2 * TRACE, WIDE), F32),
            pltpu.VMEM((rounds, cells, ROWS, WIDE), F32),
            pltpu.VMEM((rounds, cells, ROWS, WIDE), F32),
            pltpu.VMEM((rounds, cells, ROWS, WIDE), F32),
            pltpu.SemaphoreType.DMA((rounds, cells)),
            pltpu.SemaphoreType.DMA((rounds, cells)),
            pltpu.SemaphoreType.DMA((2, cells)),
            pltpu.VMEM((groups, 8, WIDE), F32),
            pltpu.VMEM((groups, 3, 8, WIDE), F32),
            pltpu.SemaphoreType.DMA((groups, 3)),
            pltpu.SemaphoreType.DMA((groups, 3)),
            pltpu.VMEM((elements, TRACE, TRACE), F32),
            pltpu.VMEM((elements, 128), F32),
            pltpu.VMEM((elements, 128), F32),
            pltpu.VMEM((elements, 128), F32),
            pltpu.VMEM((elements, 128), F32),
            pltpu.VMEM((elements, 128), F32),
            pltpu.VMEM((elements, 128), F32),
            pltpu.SemaphoreType.DMA((4,)),
            pltpu.VMEM((elements, BLOCK), F32),
        ],
        compiler_params=pltpu.CompilerParams(
            collective_id=0, has_side_effects=True, vmem_limit_bytes=62 * 1024 * 1024
        ),
    )(inv, vector, lift_maps.transpose(0, 2, 1), flat, orient.T, pick)
    return result


def solution(mesh):
    in_specs = (
        P("stream", "cross", None),
        P("stream", "cross", None, None),
        P(),
        P("stream", "cross", None, None, None, None),
        P("stream", "cross"),
    )
    out_specs = P("stream", "cross", None)
    return jax.shard_map(
        functools.partial(on_device, mesh.shape["cross"], mesh.shape["stream"]),
        mesh=mesh, in_specs=in_specs, out_specs=out_specs, check_vma=False,
    )
```

```python
import functools

import jax
import jax.numpy as jnp
import numpy as np
from jax import lax
from jax.experimental import pallas as pl
from jax.experimental.pallas import tpu as pltpu
from jax.sharding import PartitionSpec as P

ORDER = 3
EXTENT = ORDER + 1
VARS = 5
FACE = EXTENT * EXTENT
TRACE = VARS * FACE
BLOCK = VARS * FACE * EXTENT
HALF = BLOCK // 2
SLOTS = (0, EXTENT - 1) + tuple(range(1, EXTENT - 1))
WIDE = 256
ROWS = TRACE + 8
F32 = jnp.float32
BF16 = jnp.bfloat16


def split(value):
    high = value.astype(BF16)
    return high, (value - high.astype(F32)).astype(BF16)


def product(left, right, transposed=False):
    dims = (((1,), (1 if transposed else 0,)), ((), ()))
    dot = functools.partial(lax.dot_general, dimension_numbers=dims, preferred_element_type=F32)
    left_high, left_low = left
    right_high, right_low = right
    return dot(left_high, right_high) + (dot(left_high, right_low) + dot(left_low, right_high))


def spread(value):
    wide = BLOCK - BLOCK % WIDE
    high_part, low_part = split(value)
    none = jnp.zeros((value.shape[0], WIDE - 3 * (BLOCK - wide)), BF16)
    return (high_part[:, :wide], low_part[:, :wide]), (high_part[:, wide:], low_part[:, wide:]), none


def pack_left(value):
    (body_high, body_low), (tail_high, tail_low), none = spread(value)
    return jnp.concatenate([body_high, body_high, body_low, tail_high, tail_high, tail_low, none], axis=1)


def pack_right(value):
    (body_high, body_low), (tail_high, tail_low), none = spread(value)
    return jnp.concatenate([body_high, body_low, body_high, tail_high, tail_low, tail_high, none], axis=1)


def against(left, right):
    return lax.dot_general(left, right, (((1,), (1,)), ((), ())), preferred_element_type=F32)


def faced(face, value):
    high_part, low_part = split(value)
    return jnp.dot(
        face, jnp.concatenate([high_part, low_part, high_part], axis=0), preferred_element_type=F32
    )


def multiply(left, right):
    return product(split(left), split(right))


def lanes(shape):
    return lax.broadcasted_iota(jnp.int32, shape, 1)


def rows(shape):
    return lax.broadcasted_iota(jnp.int32, shape, 0)


def keep(mask, value):
    return jnp.where(mask, value, 0.0)


def low(value):
    return keep(lanes(value.shape) < TRACE, value)


def high(value):
    lane = lanes(value.shape)
    return keep((lane >= TRACE) & (lane < 2 * TRACE), value)


def below(value):
    return jnp.concatenate([jnp.zeros((TRACE, value.shape[1]), F32), value], axis=0)


def to_low(value):
    return low(pltpu.roll(value, WIDE - 2 * TRACE, 1))


def join(left, right):
    lane = lanes((TRACE, WIDE))
    through = below(keep(lane < 2 * TRACE, right[:TRACE]))
    first = multiply(left[:, : 2 * TRACE], through)
    lane_all = lanes((ROWS, WIDE))
    row_all = rows((ROWS, WIDE))
    first = first + keep((lane_all >= 2 * TRACE) | (row_all >= TRACE), right)
    back = left[:TRACE]
    through = jnp.concatenate(
        [to_low(back), jnp.zeros((TRACE, WIDE), F32), keep(lane >= 2 * TRACE, back)], axis=0
    )
    second = multiply(first[:, : 3 * TRACE], through)
    middle = (lane_all >= TRACE) & (lane_all < 2 * TRACE)
    return first, second + keep(middle, first) + keep(lane_all < TRACE, left)


def apply(column, matrix):
    return jnp.sum(column * matrix, axis=0, keepdims=True)


def stack(parts):
    total = jnp.zeros((8, parts[0].shape[1]), F32)
    row = rows(total.shape)
    for index, part in enumerate(parts):
        total = jnp.where(row == index, jnp.broadcast_to(part, total.shape), total)
    return total


def each(z, matrices):
    pieces = split(z[:, : 2 * TRACE])
    row = rows((8, WIDE))
    total = jnp.zeros((8, WIDE), F32)
    for index, matrix in enumerate(matrices):
        total = jnp.where(row == index, product(pieces, split(matrix)), total)
    return total


def kernel(
    layers, cells, width, rounds,
    inv, vector_source, lift_maps, jacobian_source, orient_source, pick_source, out,
    blocks, block_sem, lifts, lift_sem, pick, pick_sem, vector, jacobians, orient, input_sem, vecs, jac_rows, packed, near,
    ends, sides, inner, full, y, x, entry, climb, climb_got, climb_send, climb_recv, reach, zmat, drop, firsts,
    mine, theirs, send_sem, recv_sem, tail_sems, z_mine, z_theirs, z_send, z_recv,
    turns, traces, backs, got_high, got_back, from_left, from_right, cross_sems, natural,
):
    elements = layers * cells
    place = lax.axis_index("stream")
    column_at = lax.axis_index("cross")
    last = layers - 1
    vec_rows = vecs.shape[0]

    def at(layer, c):
        return layer * cells + c

    order = [at(layer, c) for c in range(cells) for layer in range(layers)]

    lift_copies = [
        pltpu.make_async_copy(lift_maps.at[2 * h : 2 * h + 2], lifts.at[2 * h : 2 * h + 2], lift_sem.at[h])
        for h in range(2)
    ]

    def block_copies(e, slots):
        return [
            pltpu.make_async_copy(inv.at[e, :, SLOTS[s]], blocks.at[e, s], block_sem.at[e, s]) for s in slots
        ]

    early, late = (0, 1), tuple(range(2, EXTENT))
    def column_of(c):
        return [at(layer, c) for layer in range(layers)]

    def fetch(members, slots):
        for e in members:
            for copy in block_copies(e, slots):
                copy.start()

    def ready(members, slots):
        for e in members:
            for copy in block_copies(e, slots):
                copy.wait()

    input_copies = [
        pltpu.make_async_copy(jacobian_source, jacobians, input_sem.at[0]),
        pltpu.make_async_copy(vector_source, vector, input_sem.at[1]),
        pltpu.make_async_copy(orient_source, orient, input_sem.at[2]),
    ]
    lift_copies[0].start()
    input_copies[1].start()
    input_copies[0].start()
    fetch(column_of(0), early)
    input_copies[2].start()
    pick_copy = pltpu.make_async_copy(pick_source, pick, pick_sem.at[0])

    bits = [lax.rem(place // (1 << k), 2) for k in range(rounds)]
    partners = [place + (1 - 2 * bits[k]) * (1 << k) for k in range(rounds)]
    paired = min(2, rounds)
    groups = [tuple(range(paired))] + [(k,) for k in range(paired, rounds)]
    friends = []
    for group in groups:
        near_one, far_one = partners[group[0]], partners[group[-1]]
        friends.append([near_one, far_one, near_one + far_one - place] if len(group) == 2 else [near_one])
    met_count = sum(len(friend) for friend in friends)
    barrier = pltpu.get_barrier_semaphore()
    for friend in friends:
        for partner in friend:
            pl.semaphore_signal(barrier, inc=1, device_id=(partner, column_at), device_id_type=pl.DeviceIdType.MESH)

    @pl.when(column_at > 0)
    def _():
        pl.semaphore_signal(barrier, inc=1, device_id=(place, column_at - 1), device_id_type=pl.DeviceIdType.MESH)

    @pl.when(column_at < width - 1)
    def _():
        pl.semaphore_signal(barrier, inc=1, device_id=(place, column_at + 1), device_id_type=pl.DeviceIdType.MESH)

    vecs[...] = jnp.zeros_like(vecs)
    jac_rows[...] = jnp.zeros_like(jac_rows)
    backs[...] = jnp.zeros_like(backs)

    def spread_jacobians(c):
        for e in column_of(c):
            for v in range(VARS):
                for w in range(VARS):
                    jac_rows[e, w, :4, v * FACE : (v + 1) * FACE] = jacobians[e, v, w]
            for w in range(VARS):
                value = jac_rows[e, w]
                jac_rows[e, w] = value + pltpu.roll(value, TRACE, 1) + pltpu.roll(value, 2 * TRACE, 1)


    row_face = rows((TRACE, TRACE))
    lane_face = lanes((TRACE, TRACE))
    row_wide = lax.rem(rows((TRACE, WIDE)), FACE)
    lane_wide = lax.rem(lanes((TRACE, WIDE)), FACE)
    same = row_wide == lane_wide
    leading = lanes((TRACE, WIDE)) < 2 * TRACE
    lane_line = lax.rem(lanes((1, WIDE)), FACE)
    eye = rows((TRACE, WIDE)) == lanes((TRACE, WIDE))
    eye_low = eye.astype(F32)
    eye_high = (rows((TRACE, WIDE)) + TRACE == lanes((TRACE, WIDE))).astype(F32)
    first_row = rows((8, WIDE)) == 0

    def source_of(code, node_index):
        first = lax.div(node_index, EXTENT)
        second = node_index - first * EXTENT
        first, second = (
            first + lax.rem(code, 2) * (second - first),
            second + lax.rem(code, 2) * (first - second),
        )
        first = first + lax.rem(code // 2, 2) * (EXTENT - 1 - 2 * first)
        second = second + lax.rem(code // 4, 2) * (EXTENT - 1 - 2 * second)
        return first * EXTENT + second

    def face(e, m, chosen):
        tall = jnp.concatenate(
            [jnp.broadcast_to(jac_rows[e, w, m : m + 1, :], (FACE, WIDE)) for w in range(VARS)],
            axis=0,
        )
        value = keep(chosen, tall)
        value = jnp.where(leading, value, value - value.astype(BF16).astype(F32))
        return value[:, : 3 * TRACE].astype(BF16)

    def half(e, h):
        return pack_right(blocks[e, 2 * h : 2 * h + 2].reshape(HALF, BLOCK))

    def ending(e, h, through):
        ends[e, h, TRACE:, :HALF] = -faced(face(e, 0, same), through[:TRACE])
        ends[e, h, :TRACE, :HALF] = -faced(face(e, 1, same), through[TRACE : 2 * TRACE])

    vec_at, rest_at = 2 * TRACE, 2 * TRACE + vec_rows
    lift_copies[0].wait()
    packed[:vec_at] = pack_left(lifts[0:2].reshape(2 * TRACE, BLOCK))
    input_copies[1].wait()
    for e in range(elements):
        vecs[e : e + 1, :] = vector[e // cells, e % cells : e % cells + 1, :]
    packed[vec_at:rest_at] = pack_left(vecs[...])
    input_copies[0].wait()

    def passing(e):
        block = half(e, 0)
        near[e] = block
        through = against(packed[:rest_at], block)
        y[0, e : e + 1, :HALF] = through[vec_at + e : vec_at + e + 1]
        return through

    held = {}

    def rest_pass(e):
        held[e] = against(packed[...], half(e, 1)), against(packed[rest_at:], near[e])

    def rest_end(e):
        through, beside = held.pop(e)
        y[1, e : e + 1, :HALF] = through[vec_at + e : vec_at + e + 1]
        ending(e, 1, through)
        chosen = row_wide == source_of(orient[e % cells, e // cells], lane_line)
        faces = face(e, 2, chosen), face(e, 3, same)
        for h, value in enumerate((beside, through[rest_at:])):
            for m in range(2):
                sides[e, h, m * TRACE : (m + 1) * TRACE, :HALF] = faced(
                    faces[m], value[m * TRACE : (m + 1) * TRACE]
                )

    def finish(e):
        for h in range(2):
            full[e, h] = product(split(inner[e, :, : 2 * TRACE]), split(ends[e, h]))

    def chain(c):
        up = [ends[at(layer, c), 0, TRACE:] for layer in range(layers)]
        down = [ends[at(layer, c), 0, :TRACE] for layer in range(layers)]

        def bottom(layer):
            e = at(layer, c)
            return keep(first_row, jnp.broadcast_to(y[0, e : e + 1, :], (8, WIDE)))

        forward = [jnp.concatenate([up[0], bottom(0)], axis=0)]
        for layer in range(1, layers):
            step = multiply(forward[-1][:, : 2 * TRACE], below(up[layer]))
            forward.append(step + below(bottom(layer)))
            yield
        none = jnp.zeros((ROWS, WIDE), F32)
        backward = jnp.concatenate([eye_low, none], axis=0)
        for layer in reversed(range(layers)):
            before = forward[layer - 1] if layer else jnp.concatenate([eye_high, none[TRACE:]], axis=0)
            inner[at(layer, c)] = backward + below(high(before))
            if layer == last:
                backward = low(jnp.concatenate([down[layer], forward[layer]], axis=0))
            else:
                backward = low(multiply(backward[:, :TRACE], down[layer]) + below(forward[layer]))
                yield
        whole = backward[TRACE:] + high(forward[last])
        extra = pltpu.roll(backward[:TRACE], 2 * TRACE, 1)
        mine[0, c, TRACE:] = whole[TRACE:]
        mine[0, c, :TRACE] = whole[:TRACE] + extra

    def responses(c):
        behind = eye_low
        reach_low, after = [], []
        for layer in range(layers):
            reach_low.append(behind)
            e = at(layer, c)
            pair = jnp.concatenate([ends[e, 0, TRACE:], ends[e, 0, :TRACE]], axis=0)
            if layer == 0:
                both = low(pair)
            else:
                both = low(multiply(pair[:, :TRACE], behind))
                yield
            after.append(both[:TRACE])
            behind = both[TRACE:]
        ahead = eye_high
        for layer in reversed(range(layers)):
            e = at(layer, c)
            zmat[e, :TRACE] = reach_low[layer]
            zmat[e, TRACE:] = ahead
            if layer:
                if layer == last:
                    ahead = high(ends[e, 0, TRACE:]) + after[layer]
                else:
                    ahead = multiply(ends[e, 0, TRACE:, : 2 * TRACE], below(ahead)) + after[layer]
                    yield

    def ordered(k, c):
        flag = bits[k] == 1
        ours, other = mine[k, c], theirs[k, c]
        return jnp.where(flag, other, ours), jnp.where(flag, ours, other)

    def reaching(k, c, first):
        flag = bits[k] == 1
        if k == 0:
            near, far = eye_low, low(first)
            ahead = eye_high
        else:
            near, ahead = entry[k, c, :TRACE], entry[k, c, TRACE : 2 * TRACE]
            far = multiply(first[:, :TRACE], near)
        reach[k, c, :TRACE] = jnp.where(flag, 0.0, near)
        reach[k, c, TRACE:] = jnp.where(flag, ahead, far)

    def reach_level(k, c):
        other = jnp.where(bits[k] == 1, mine[k, c, :TRACE, :128], theirs[k, c, :TRACE, :128])
        reaching(k, c, jnp.concatenate([other, jnp.zeros((TRACE, WIDE - 128), F32)], axis=1))

    def level(k, c):
        left, right = ordered(k, c)
        flag = bits[k] == 1
        first = firsts[k, c]
        step = jnp.concatenate(
            [
                jnp.where(flag, eye_low, to_low(right[:TRACE])),
                jnp.where(flag, high(left[:TRACE]), low(first[:TRACE]) + eye_high),
                jnp.where(flag, high(left[TRACE:]), low(first[TRACE:])),
            ],
            axis=0,
        )
        if k == 0:
            entry[1, c] = step
        else:
            old = entry[k, c]
            moved = multiply(step[:, : 2 * TRACE], old[: 2 * TRACE])
            entry[k + 1, c, : 2 * TRACE] = moved[: 2 * TRACE]
            entry[k + 1, c, 2 * TRACE :] = moved[2 * TRACE :] + old[2 * TRACE :]

    def climbing(k, c):
        left, right = ordered(k, c)
        back = left[:TRACE]
        turned = low(multiply(right[:TRACE, :TRACE], to_low(back)))
        climb[k, c] = turned + high(right[:TRACE]) + keep(lanes((TRACE, WIDE)) >= 2 * TRACE, back)

    def climber(packed_climb):
        return jnp.concatenate([to_low(packed_climb), packed_climb], axis=0)

    alike = lax.div(row_face, FACE) == lax.div(lane_face, FACE)
    small_row = rows((FACE, TRACE))
    small_lane = lax.rem(lanes((FACE, TRACE)), FACE)

    def turn(e):
        chosen = (source_of(orient[e % cells, e // cells], small_row) == small_lane).astype(F32)
        turns[e] = keep(alike, jnp.concatenate([chosen] * VARS, axis=0))

    def remote(source, target, send, recv, device):
        return pltpu.make_async_remote_copy(
            src_ref=source, dst_ref=target, send_sem=send, recv_sem=recv,
            device_id=device, device_id_type=pl.DeviceIdType.MESH,
        )

    sent = []
    pending = {}
    climb_copies = {}

    def dispatch(k, c):
        device = (partners[k], column_at)
        send, recv = send_sem.at[k, c], recv_sem.at[k, c]
        if k < rounds - 1:
            pending[k, c] = [remote(mine.at[k, c], theirs.at[k, c], send, recv, device)]
        else:
            one, two = pl.ds(0, 128), pl.ds(128, 128)
            foot = pl.ds(TRACE, 8)
            pending[k, c] = [
                remote(mine.at[k, c, :, one], theirs.at[k, c, :, one], send, recv, device),
                remote(
                    mine.at[k, c, foot, two], theirs.at[k, c, foot, two],
                    tail_sems.at[0, c], tail_sems.at[1, c], device,
                ),
            ]
        for copy in pending[k, c]:
            copy.start()
            sent.append(copy)

    sides_met = jnp.minimum(column_at, 1) + jnp.minimum(width - 1 - column_at, 1)
    ready(column_of(0), early)
    for c in range(1, cells):
        fetch(column_of(c), early)
    lift_copies[1].start()
    fetch(order, late)
    pick_copy.start()
    throughs = [passing(e) for e in column_of(0)]
    spread_jacobians(0)
    for e, through in zip(column_of(0), throughs):
        ending(e, 0, through)
    for c in range(cells):
        steps = chain(c)
        if c + 1 < cells:
            ready(column_of(c + 1), early)
            spread_jacobians(c + 1)
            throughs = []
            for e in column_of(c + 1):
                next(steps, None)
                throughs.append(passing(e))
            for e, through in zip(column_of(c + 1), throughs):
                next(steps, None)
                ending(e, 0, through)
        for _ in steps:
            pass
        if c == 0:
            pl.semaphore_wait(barrier, met_count + sides_met)
        dispatch(0, c)

    lift_copies[1].wait()
    input_copies[2].wait()
    packed[rest_at:] = pack_left(lifts[2:4].reshape(2 * TRACE, BLOCK))
    ready(order, late)
    if rounds == 1:
        for c in range(cells):
            entry[0, c] = jnp.concatenate([eye_low, eye_high, jnp.zeros((8, WIDE), F32)], axis=0)

    answering = [responses(c) for c in range(cells)]

    def stage(index):
        if index < elements:
            rest_pass(order[index])
        if 0 < index <= elements:
            rest_end(order[index - 1])
        if index > 1:
            finish(order[index - 2])
        for steps in answering:
            next(steps, None)

    def finish_answers():
        for steps in answering:
            for _ in steps:
                pass

    def compose(e):
        drop[e] = multiply(sides[e, 0, :, :HALF], zmat[e])

    tasks = []

    def later(cost, function, *values):
        tasks.append((cost, functools.partial(function, *values)))

    for index in range(elements + 2):
        later(0.65, stage, index)
    later(0.05, finish_answers)
    for e in range(elements):
        later(0.03, turn, e)
    for e in range(elements):
        later(0.1, compose, e)

    def work(budget):
        while tasks and (budget is None or tasks[0][0] <= budget):
            cost, task = tasks.pop(0)
            task()
            if budget is not None:
                budget -= cost

    for k in range(rounds):
        for c in range(cells):
            work(None if k == rounds - 1 and c == cells - 1 else 2.0 if k == c == 0 else 0.7)
            for copy in pending[k, c]:
                copy.wait_recv()
            if k < rounds - 1:
                left, right = ordered(k, c)
                first, node = join(left, right)
                mine[k + 1, c] = node
                dispatch(k + 1, c)
                firsts[k, c] = first
                level(k, c)
                if k == 0 and c == cells - 1:
                    for other in range(cells):
                        climbing(k, other)
                        copy = remote(
                            climb.at[k, other], climb_got.at[k, other],
                            climb_send.at[k, other], climb_recv.at[k, other], (partners[k + 1], column_at),
                        )
                        copy.start()
                        sent.append(copy)
                        climb_copies[k, other] = copy
    work(None)

    top = rounds - 1
    top_flag = bits[top] == 1

    def meet(z_ours, z_other, flag):
        z_left, z_right = jnp.where(flag, z_other, z_ours), jnp.where(flag, z_ours, z_other)
        return low(z_right) + high(z_left), low(z_left) + high(z_right)

    z_ours = stack([mine[top, c, TRACE : TRACE + 1] for c in range(cells)])
    z_other = stack([theirs[top, c, TRACE : TRACE + 1] for c in range(cells)])
    met, _ = meet(z_ours, z_other, top_flag)
    turned = each(met, [below(low(theirs[top, c, :TRACE])) for c in range(cells)])
    arrived = jnp.where(top_flag, high(met), low(met + turned))
    z_in = each(arrived, [entry[top, c, : 2 * TRACE] for c in range(cells)]) + stack(
        [entry[top, c, 2 * TRACE : 2 * TRACE + 1] for c in range(cells)]
    )
    column = z_in.T
    for layer in range(layers):
        for c in range(cells):
            e = at(layer, c)
            for h in range(2):
                x[h, e : e + 1, :] = (
                    y[h, e : e + 1, :]
                    + full[e, h, 2 * TRACE : 2 * TRACE + 1]
                    + apply(column[: 2 * TRACE, c : c + 1], full[e, h, : 2 * TRACE])
                )

    pick_copy.wait()
    cross = jnp.zeros((elements, WIDE), F32)
    for h in range(2):
        x_high, x_low = split(x[h, :, :HALF])
        cross = cross + (
            jnp.dot(x_high, pick[h], preferred_element_type=F32)
            + jnp.dot(x_low, pick[h], preferred_element_type=F32)
        )
    traces[...] = cross[:, 128:]
    column = cross[:, :128].T
    for e in range(elements):
        backs[e : e + 1, :TRACE] = apply(column[:TRACE, e : e + 1], turns[e])
    up = remote(traces, got_high, cross_sems.at[0], cross_sems.at[1], (place, lax.rem(column_at + 1, width)))
    down = remote(backs, got_back, cross_sems.at[2], cross_sems.at[3], (place, lax.rem(column_at + width - 1, width)))

    @pl.when(column_at < width - 1)
    def _():
        up.start()

    @pl.when(column_at > 0)
    def _():
        down.start()

    def prepare(g):
        for k in groups[g]:
            for c in range(cells):
                reach_level(k, c)
                if 0 < k < top:
                    climbing(k, c)

    prepare(0)
    for layer in range(layers):
        for c in range(cells):
            e = at(layer, c)
            if c > 0:
                from_left[e : e + 1, :] = traces[e - 1 : e, :]
            if c < cells - 1:
                from_right[e : e + 1, :] = backs[e + 1 : e + 2, :]
    firsts_at = [layer * cells for layer in range(layers)]
    lasts_at = [layer * cells + cells - 1 for layer in range(layers)]

    @pl.when(column_at > 0)
    def _():
        up.wait_recv()
        for one, two in zip(firsts_at, lasts_at):
            from_left[one : one + 1, :] = got_high[two : two + 1, :]

    @pl.when(column_at == 0)
    def _():
        for one in firsts_at:
            from_left[one : one + 1, :] = jnp.zeros((1, 128), F32)

    @pl.when(column_at < width - 1)
    def _():
        down.wait_recv()
        for one, two in zip(firsts_at, lasts_at):
            from_right[two : two + 1, :] = got_back[one : one + 1, :]

    @pl.when(column_at == width - 1)
    def _():
        for two in lasts_at:
            from_right[two : two + 1, :] = jnp.zeros((1, 128), F32)

    left_columns = from_left[...].T
    right_columns = from_right[...].T

    def loaded(e, h):
        return y[h, e : e + 1, :] - (
            apply(left_columns[:TRACE, e : e + 1], sides[e, h, :TRACE])
            + apply(right_columns[:TRACE, e : e + 1], sides[e, h, TRACE:])
        )

    def dropped(e):
        return apply(left_columns[:TRACE, e : e + 1], drop[e, :TRACE]) + apply(
            right_columns[:TRACE, e : e + 1], drop[e, TRACE:]
        )

    z_mine[0] = stack([
        mine[0, c, TRACE : TRACE + 1] - functools.reduce(jnp.add, [dropped(at(layer, c)) for layer in range(layers)])
        for c in range(cells)
    ])

    state = {}

    def gathered(layer):
        return stack([y[0, at(layer, c) : at(layer, c) + 1, :] for c in range(cells)])

    def local_sweeps():
        for e in range(elements):
            y[0, e : e + 1, :] = loaded(e, 0)
        forward = [gathered(0)]
        for layer in range(1, layers):
            step = each(forward[-1], [below(ends[at(layer, c), 0, TRACE:]) for c in range(cells)])
            forward.append(step + gathered(layer))
        backward = jnp.zeros((8, WIDE), F32)
        for layer in reversed(range(layers)):
            before = high(forward[layer - 1]) if layer else jnp.zeros((8, WIDE), F32)
            state[layer] = backward + before
            if layer == last:
                backward = low(forward[layer])
            elif layer:
                inverse = [
                    jnp.concatenate([ends[at(layer, c), 0, :TRACE], jnp.zeros((TRACE, WIDE), F32)], axis=0)
                    for c in range(cells)
                ]
                backward = low(each(backward, inverse) + forward[layer])

    def local_rest():
        for e in range(elements):
            y[1, e : e + 1, :] = loaded(e, 1)

    def local_settle():
        local_rest()
        for layer in range(layers):
            column = state[layer].T
            for c in range(cells):
                e = at(layer, c)
                for h in range(2):
                    x[h, e : e + 1, :] = y[h, e : e + 1, :] + apply(column[: 2 * TRACE, c : c + 1], ends[e, h])

    for task in (local_sweeps, local_settle):
        later(0, task)
    z_in = jnp.zeros((8, WIDE), F32)
    for g, group in enumerate(groups):
        copies = [
            remote(z_mine.at[g], z_theirs.at[g, i], z_send.at[g, i], z_recv.at[g, i], (partner, column_at))
            for i, partner in enumerate(friends[g])
        ]
        for copy in copies:
            copy.start()
            sent.append(copy)
        if g + 1 < len(groups):
            prepare(g + 1)
            tasks.pop(0)[1]() if tasks else None
        else:
            work(None)
        k = group[0]
        if len(group) == 2:
            for c in range(cells):
                climb_copies[k, c].wait_recv()
        for copy in copies:
            copy.wait_recv()
        flag = bits[k] == 1
        met, kept = meet(z_mine[g], z_theirs[g, 0], flag)
        z_in = z_in + each(met, [reach[k, c] for c in range(cells)])
        if len(group) == 2:
            both, stays = meet(z_theirs[g, 1], z_theirs[g, 2], flag)
            ours = kept + each(met, [climber(climb[k, c]) for c in range(cells)])
            other = stays + each(both, [climber(climb_got[k, c]) for c in range(cells)])
            k = group[1]
            met, kept = meet(ours, other, bits[k] == 1)
            z_in = z_in + each(met, [reach[k, c] for c in range(cells)])
        if k < top:
            z_mine[g + 1] = kept + each(met, [climber(climb[k, c]) for c in range(cells)])

    column = z_in.T
    for layer in range(layers):
        for c in range(cells):
            e = at(layer, c)
            for h in range(2):
                x[h, e : e + 1, :] = x[h, e : e + 1, :] + apply(
                    column[: 2 * TRACE, c : c + 1], full[e, h, : 2 * TRACE]
                )
    for slot, i in enumerate(SLOTS):
        for v in range(VARS):
            target = (v * EXTENT + i) * FACE
            source = (slot % 2) * TRACE + v * FACE
            natural[:, target : target + FACE] = x[slot // 2, :, source : source + FACE]
    for layer in range(layers):
        out[layer] = natural[layer * cells : (layer + 1) * cells, :]

    for copy in sent:
        copy.wait_send()

    @pl.when(column_at < width - 1)
    def _():
        up.wait_send()

    @pl.when(column_at > 0)
    def _():
        down.wait_send()


def picker():
    table = np.zeros((2, HALF, WIDE), np.float32)
    for slot, i in enumerate(SLOTS):
        for v in range(VARS):
            for k in range(EXTENT):
                source = (slot % 2) * TRACE + v * FACE + k
                target = v * FACE + i * EXTENT + k
                table[slot // 2, source, target] = 1.0
                table[slot // 2, source + (EXTENT - 1) * EXTENT, 128 + target] = 1.0
    return table


def on_device(width, count, vector, inverses, lift_maps, jacobians, orient):
    layers, cells = vector.shape[:2]
    elements = layers * cells
    rounds = count.bit_length() - 1
    inv = inverses.reshape(elements, VARS, EXTENT, FACE, BLOCK)
    flat = jacobians.transpose(0, 1, 3, 4, 2, 5).reshape(elements, VARS, VARS, 4, FACE)
    pick = jnp.asarray(picker(), BF16)
    vec_rows = -(-elements // 16) * 16
    depth = 4 * TRACE + vec_rows
    vmem = pl.BlockSpec(memory_space=pltpu.VMEM)
    hbm = pl.BlockSpec(memory_space=pltpu.HBM)
    tall = 2 * TRACE + 8
    groups = max(1, rounds - 1)
    result = pl.pallas_call(
        functools.partial(kernel, layers, cells, width, rounds),
        out_shape=pltpu.VMEM((layers, cells, BLOCK), F32),
        in_specs=[hbm] * 6,
        out_specs=vmem,
        scratch_shapes=[
            pltpu.VMEM((elements, EXTENT, VARS, FACE, BLOCK), F32),
            pltpu.SemaphoreType.DMA((elements, EXTENT)),
            pltpu.VMEM((4, TRACE, BLOCK), F32),
            pltpu.SemaphoreType.DMA((2,)),
            pltpu.VMEM((2, HALF, WIDE), BF16),
            pltpu.SemaphoreType.DMA((1,)),
            pltpu.VMEM((layers, cells, BLOCK), F32),
            pltpu.VMEM((elements, VARS, VARS, 4, FACE), F32),
            pltpu.SMEM((cells, layers), jnp.int32),
            pltpu.SemaphoreType.DMA((3,)),
            pltpu.VMEM((vec_rows, BLOCK), F32),
            pltpu.VMEM((elements, VARS, 8, WIDE), F32),
            pltpu.VMEM((depth, 4 * WIDE), BF16),
            pltpu.VMEM((elements, HALF, 4 * WIDE), BF16),
            pltpu.VMEM((elements, 2, 2 * TRACE, WIDE), F32),
            pltpu.VMEM((elements, 2, 2 * TRACE, WIDE), F32),
            pltpu.VMEM((elements, tall, WIDE), F32),
            pltpu.VMEM((elements, 2, tall, WIDE), F32),
            pltpu.VMEM((2, elements, WIDE), F32),
            pltpu.VMEM((2, elements, WIDE), F32),
            pltpu.VMEM((rounds, cells, tall, WIDE), F32),
            pltpu.VMEM((rounds, cells, TRACE, WIDE), F32),
            pltpu.VMEM((rounds, cells, TRACE, WIDE), F32),
            pltpu.SemaphoreType.DMA((rounds, cells)),
            pltpu.SemaphoreType.DMA((rounds, cells)),
            pltpu.VMEM((rounds, cells, 2 * TRACE, WIDE), F32),
            pltpu.VMEM((elements, 2 * TRACE, WIDE), F32),
            pltpu.VMEM((elements, 2 * TRACE, WIDE), F32),
            pltpu.VMEM((rounds, cells, ROWS, WIDE), F32),
            pltpu.VMEM((rounds, cells, ROWS, WIDE), F32),
            pltpu.VMEM((rounds, cells, ROWS, WIDE), F32),
            pltpu.SemaphoreType.DMA((rounds, cells)),
            pltpu.SemaphoreType.DMA((rounds, cells)),
            pltpu.SemaphoreType.DMA((2, cells)),
            pltpu.VMEM((groups, 8, WIDE), F32),
            pltpu.VMEM((groups, 3, 8, WIDE), F32),
            pltpu.SemaphoreType.DMA((groups, 3)),
            pltpu.SemaphoreType.DMA((groups, 3)),
            pltpu.VMEM((elements, TRACE, TRACE), F32),
            pltpu.VMEM((elements, 128), F32),
            pltpu.VMEM((elements, 128), F32),
            pltpu.VMEM((elements, 128), F32),
            pltpu.VMEM((elements, 128), F32),
            pltpu.VMEM((elements, 128), F32),
            pltpu.VMEM((elements, 128), F32),
            pltpu.SemaphoreType.DMA((4,)),
            pltpu.VMEM((elements, BLOCK), F32),
        ],
        compiler_params=pltpu.CompilerParams(
            collective_id=0, has_side_effects=True, vmem_limit_bytes=62 * 1024 * 1024
        ),
    )(inv, vector, lift_maps.transpose(0, 2, 1), flat, orient.T, pick)
    return result


def solution(mesh):
    in_specs = (
        P("stream", "cross", None),
        P("stream", "cross", None, None),
        P(),
        P("stream", "cross", None, None, None, None),
        P("stream", "cross"),
    )
    out_specs = P("stream", "cross", None)
    return jax.shard_map(
        functools.partial(on_device, mesh.shape["cross"], mesh.shape["stream"]),
        mesh=mesh, in_specs=in_specs, out_specs=out_specs, check_vma=False,
    )
```

```python
import functools

import jax
import jax.numpy as jnp
import numpy as np
from jax import lax
from jax.experimental import pallas as pl
from jax.experimental.pallas import tpu as pltpu
from jax.sharding import PartitionSpec as P

ORDER = 3
EXTENT = ORDER + 1
VARS = 5
FACE = EXTENT * EXTENT
TRACE = VARS * FACE
BLOCK = VARS * FACE * EXTENT
HALF = BLOCK // 2
SLOTS = (0, EXTENT - 1) + tuple(range(1, EXTENT - 1))
WIDE = 256
ROWS = TRACE + 8
F32 = jnp.float32
BF16 = jnp.bfloat16


def split(value):
    high = value.astype(BF16)
    return high, (value - high.astype(F32)).astype(BF16)


def product(left, right, transposed=False):
    dims = (((1,), (1 if transposed else 0,)), ((), ()))
    dot = functools.partial(lax.dot_general, dimension_numbers=dims, preferred_element_type=F32)
    left_high, left_low = left
    right_high, right_low = right
    return dot(left_high, right_high) + (dot(left_high, right_low) + dot(left_low, right_high))


def spread(value):
    wide = BLOCK - BLOCK % WIDE
    high_part, low_part = split(value)
    none = jnp.zeros((value.shape[0], WIDE - 3 * (BLOCK - wide)), BF16)
    return (high_part[:, :wide], low_part[:, :wide]), (high_part[:, wide:], low_part[:, wide:]), none


def pack_left(value):
    (body_high, body_low), (tail_high, tail_low), none = spread(value)
    return jnp.concatenate([body_high, body_high, body_low, tail_high, tail_high, tail_low, none], axis=1)


def pack_right(value):
    (body_high, body_low), (tail_high, tail_low), none = spread(value)
    return jnp.concatenate([body_high, body_low, body_high, tail_high, tail_low, tail_high, none], axis=1)


def against(left, right):
    return lax.dot_general(left, right, (((1,), (1,)), ((), ())), preferred_element_type=F32)


def faced(face, value):
    high_part, low_part = split(value)
    return jnp.dot(
        face, jnp.concatenate([high_part, low_part, high_part], axis=0), preferred_element_type=F32
    )


def multiply(left, right):
    return product(split(left), split(right))


def lanes(shape):
    return lax.broadcasted_iota(jnp.int32, shape, 1)


def rows(shape):
    return lax.broadcasted_iota(jnp.int32, shape, 0)


def keep(mask, value):
    return jnp.where(mask, value, 0.0)


def low(value):
    return keep(lanes(value.shape) < TRACE, value)


def high(value):
    lane = lanes(value.shape)
    return keep((lane >= TRACE) & (lane < 2 * TRACE), value)


def below(value):
    return jnp.concatenate([jnp.zeros((TRACE, value.shape[1]), F32), value], axis=0)


def to_low(value):
    return low(pltpu.roll(value, WIDE - 2 * TRACE, 1))


def join(left, right):
    lane = lanes((TRACE, WIDE))
    through = below(keep(lane < 2 * TRACE, right[:TRACE]))
    first = multiply(left[:, : 2 * TRACE], through)
    lane_all = lanes((ROWS, WIDE))
    row_all = rows((ROWS, WIDE))
    first = first + keep((lane_all >= 2 * TRACE) | (row_all >= TRACE), right)
    through = jnp.concatenate(
        [jnp.zeros((2 * TRACE, WIDE), F32), keep(lane >= 2 * TRACE, left[:TRACE])], axis=0
    )
    passed = multiply(right[:TRACE, : 3 * TRACE], through)
    upper = high(first) + jnp.concatenate([passed, jnp.zeros((8, WIDE), F32)], axis=0)
    return first, upper


def join_low(left, first):
    return multiply(first[:, :TRACE], to_low(left[:TRACE])) + low(left)


def apply(column, matrix):
    return jnp.sum(column * matrix, axis=0, keepdims=True)


def stack(parts):
    total = jnp.zeros((8, parts[0].shape[1]), F32)
    row = rows(total.shape)
    for index, part in enumerate(parts):
        total = jnp.where(row == index, jnp.broadcast_to(part, total.shape), total)
    return total


def each(z, matrices):
    pieces = split(z[:, : 2 * TRACE])
    row = rows((8, WIDE))
    total = jnp.zeros((8, WIDE), F32)
    for index, matrix in enumerate(matrices):
        total = jnp.where(row == index, product(pieces, split(matrix)), total)
    return total


def kernel(
    layers, cells, width, rounds,
    inv, vector_source, lift_maps, jacobian_source, orient_source, pick_source, out,
    blocks, block_sem, lifts, lift_sem, pick, pick_sem, vector, jacobians, orient, input_sem, vecs, jac_rows, packed, near,
    ends, sides, inner, full, y, x, entry, climb, climb_got, climb_send, climb_recv, reach, zmat, drop, firsts,
    mine, theirs, send_sem, recv_sem, z_mine, z_theirs, z_send, z_recv,
    turns, traces, backs, got_high, got_back, from_left, from_right, cross_sems, natural,
):
    elements = layers * cells
    place = lax.axis_index("stream")
    column_at = lax.axis_index("cross")
    last = layers - 1
    vec_rows = vecs.shape[0]

    def at(layer, c):
        return layer * cells + c

    order = [at(layer, c) for c in range(cells) for layer in range(layers)]

    lift_copies = [
        pltpu.make_async_copy(lift_maps.at[2 * h : 2 * h + 2], lifts.at[2 * h : 2 * h + 2], lift_sem.at[h])
        for h in range(2)
    ]

    def block_copies(e, slots):
        return [
            pltpu.make_async_copy(inv.at[e, :, SLOTS[s]], blocks.at[e, s], block_sem.at[e, s]) for s in slots
        ]

    early, late = (0, 1), tuple(range(2, EXTENT))
    def column_of(c):
        return [at(layer, c) for layer in range(layers)]

    def fetch(members, slots):
        for e in members:
            for copy in block_copies(e, slots):
                copy.start()

    def ready(members, slots):
        for e in members:
            for copy in block_copies(e, slots):
                copy.wait()

    input_copies = [
        pltpu.make_async_copy(jacobian_source, jacobians, input_sem.at[0]),
        pltpu.make_async_copy(vector_source, vector, input_sem.at[1]),
        pltpu.make_async_copy(orient_source, orient, input_sem.at[2]),
    ]
    lift_copies[0].start()
    input_copies[1].start()
    input_copies[0].start()
    fetch(column_of(0), early)
    input_copies[2].start()
    pick_copy = pltpu.make_async_copy(pick_source, pick, pick_sem.at[0])

    bits = [lax.rem(place // (1 << k), 2) for k in range(rounds)]
    partners = [place + (1 - 2 * bits[k]) * (1 << k) for k in range(rounds)]
    paired = min(2, rounds)
    groups = [tuple(range(paired))] + [(k,) for k in range(paired, rounds)]
    friends = []
    for group in groups:
        near_one, far_one = partners[group[0]], partners[group[-1]]
        friends.append([near_one, far_one, near_one + far_one - place] if len(group) == 2 else [near_one])
    met_count = sum(len(friend) for friend in friends)
    barrier = pltpu.get_barrier_semaphore()
    for friend in friends:
        for partner in friend:
            pl.semaphore_signal(barrier, inc=1, device_id=(partner, column_at), device_id_type=pl.DeviceIdType.MESH)

    @pl.when(column_at > 0)
    def _():
        pl.semaphore_signal(barrier, inc=1, device_id=(place, column_at - 1), device_id_type=pl.DeviceIdType.MESH)

    @pl.when(column_at < width - 1)
    def _():
        pl.semaphore_signal(barrier, inc=1, device_id=(place, column_at + 1), device_id_type=pl.DeviceIdType.MESH)

    vecs[...] = jnp.zeros_like(vecs)
    jac_rows[...] = jnp.zeros_like(jac_rows)
    backs[...] = jnp.zeros_like(backs)

    def spread_jacobians(c):
        for e in column_of(c):
            for v in range(VARS):
                for w in range(VARS):
                    jac_rows[e, w, :4, v * FACE : (v + 1) * FACE] = jacobians[e, v, w]
            for w in range(VARS):
                value = jac_rows[e, w]
                jac_rows[e, w] = value + pltpu.roll(value, TRACE, 1) + pltpu.roll(value, 2 * TRACE, 1)


    row_face = rows((TRACE, TRACE))
    lane_face = lanes((TRACE, TRACE))
    row_wide = lax.rem(rows((TRACE, WIDE)), FACE)
    lane_wide = lax.rem(lanes((TRACE, WIDE)), FACE)
    same = row_wide == lane_wide
    leading = lanes((TRACE, WIDE)) < 2 * TRACE
    lane_line = lax.rem(lanes((1, WIDE)), FACE)
    eye = rows((TRACE, WIDE)) == lanes((TRACE, WIDE))
    eye_low = eye.astype(F32)
    eye_high = (rows((TRACE, WIDE)) + TRACE == lanes((TRACE, WIDE))).astype(F32)
    first_row = rows((8, WIDE)) == 0

    def source_of(code, node_index):
        first = lax.div(node_index, EXTENT)
        second = node_index - first * EXTENT
        first, second = (
            first + lax.rem(code, 2) * (second - first),
            second + lax.rem(code, 2) * (first - second),
        )
        first = first + lax.rem(code // 2, 2) * (EXTENT - 1 - 2 * first)
        second = second + lax.rem(code // 4, 2) * (EXTENT - 1 - 2 * second)
        return first * EXTENT + second

    def face(e, m, chosen):
        tall = jnp.concatenate(
            [jnp.broadcast_to(jac_rows[e, w, m : m + 1, :], (FACE, WIDE)) for w in range(VARS)],
            axis=0,
        )
        value = keep(chosen, tall)
        value = jnp.where(leading, value, value - value.astype(BF16).astype(F32))
        return value[:, : 3 * TRACE].astype(BF16)

    def half(e, h):
        return pack_right(blocks[e, 2 * h : 2 * h + 2].reshape(HALF, BLOCK))

    def ending(e, h, through):
        ends[e, h, TRACE:, :HALF] = -faced(face(e, 0, same), through[:TRACE])
        ends[e, h, :TRACE, :HALF] = -faced(face(e, 1, same), through[TRACE : 2 * TRACE])

    vec_at, rest_at = 2 * TRACE, 2 * TRACE + vec_rows
    lift_copies[0].wait()
    packed[:vec_at] = pack_left(lifts[0:2].reshape(2 * TRACE, BLOCK))
    input_copies[1].wait()
    for e in range(elements):
        vecs[e : e + 1, :] = vector[e // cells, e % cells : e % cells + 1, :]
    packed[vec_at:rest_at] = pack_left(vecs[...])
    input_copies[0].wait()

    def passing(e):
        block = half(e, 0)
        near[e] = block
        through = against(packed[:rest_at], block)
        y[0, e : e + 1, :HALF] = through[vec_at + e : vec_at + e + 1]
        return through

    held = {}

    def rest_pass(e):
        held[e] = against(packed[...], half(e, 1)), against(packed[rest_at:], near[e])

    def rest_end(e):
        through, beside = held.pop(e)
        y[1, e : e + 1, :HALF] = through[vec_at + e : vec_at + e + 1]
        ending(e, 1, through)
        chosen = row_wide == source_of(orient[e % cells, e // cells], lane_line)
        faces = face(e, 2, chosen), face(e, 3, same)
        for h, value in enumerate((beside, through[rest_at:])):
            for m in range(2):
                sides[e, h, m * TRACE : (m + 1) * TRACE, :HALF] = faced(
                    faces[m], value[m * TRACE : (m + 1) * TRACE]
                )

    def finish(e):
        for h in range(2):
            full[e, h] = product(split(inner[e, :, : 2 * TRACE]), split(ends[e, h]))

    def chain(c):
        up = [ends[at(layer, c), 0, TRACE:] for layer in range(layers)]
        down = [ends[at(layer, c), 0, :TRACE] for layer in range(layers)]

        def bottom(layer):
            e = at(layer, c)
            return keep(first_row, jnp.broadcast_to(y[0, e : e + 1, :], (8, WIDE)))

        forward = [jnp.concatenate([up[0], bottom(0)], axis=0)]
        for layer in range(1, layers):
            step = multiply(forward[-1][:, : 2 * TRACE], below(up[layer]))
            forward.append(step + below(bottom(layer)))
            yield
        none = jnp.zeros((ROWS, WIDE), F32)
        backward = jnp.concatenate([eye_low, none], axis=0)
        for layer in reversed(range(layers)):
            before = forward[layer - 1] if layer else jnp.concatenate([eye_high, none[TRACE:]], axis=0)
            inner[at(layer, c)] = backward + below(high(before))
            if layer == last:
                backward = low(jnp.concatenate([down[layer], forward[layer]], axis=0))
            else:
                backward = low(multiply(backward[:, :TRACE], down[layer]) + below(forward[layer]))
                yield
        whole = backward[TRACE:] + high(forward[last])
        extra = pltpu.roll(backward[:TRACE], 2 * TRACE, 1)
        mine[0, c, TRACE:] = whole[TRACE:]
        mine[0, c, :TRACE] = whole[:TRACE] + extra

    def responses(c):
        behind = eye_low
        reach_low, after = [], []
        for layer in range(layers):
            reach_low.append(behind)
            e = at(layer, c)
            pair = jnp.concatenate([ends[e, 0, TRACE:], ends[e, 0, :TRACE]], axis=0)
            if layer == 0:
                both = low(pair)
            else:
                both = low(multiply(pair[:, :TRACE], behind))
                yield
            after.append(both[:TRACE])
            behind = both[TRACE:]
        ahead = eye_high
        for layer in reversed(range(layers)):
            e = at(layer, c)
            zmat[e, :TRACE] = reach_low[layer]
            zmat[e, TRACE:] = ahead
            if layer:
                if layer == last:
                    ahead = high(ends[e, 0, TRACE:]) + after[layer]
                else:
                    ahead = multiply(ends[e, 0, TRACE:, : 2 * TRACE], below(ahead)) + after[layer]
                    yield

    def ordered(k, c):
        flag = bits[k] == 1
        ours, other = mine[k, c], theirs[k, c]
        return jnp.where(flag, other, ours), jnp.where(flag, ours, other)

    def reaching(k, c, first):
        flag = bits[k] == 1
        if k == 0:
            near, far = eye_low, low(first)
            ahead = eye_high
        else:
            near, ahead = entry[k, c, :TRACE], entry[k, c, TRACE : 2 * TRACE]
            far = multiply(first[:, :TRACE], near)
        reach[k, c, :TRACE] = jnp.where(flag, 0.0, near)
        reach[k, c, TRACE:] = jnp.where(flag, ahead, far)

    def reach_level(k, c):
        other = jnp.where(bits[k] == 1, mine[k, c, :TRACE, :128], theirs[k, c, :TRACE, :128])
        reaching(k, c, jnp.concatenate([other, jnp.zeros((TRACE, WIDE - 128), F32)], axis=1))

    def level(k, c):
        left, right = ordered(k, c)
        flag = bits[k] == 1
        first = firsts[k, c]
        step = jnp.concatenate(
            [
                jnp.where(flag, eye_low, to_low(right[:TRACE])),
                jnp.where(flag, high(left[:TRACE]), low(first[:TRACE]) + eye_high),
                jnp.where(flag, high(left[TRACE:]), low(first[TRACE:])),
            ],
            axis=0,
        )
        if k == 0:
            entry[1, c] = step
        else:
            old = entry[k, c]
            moved = multiply(step[:, : 2 * TRACE], old[: 2 * TRACE])
            entry[k + 1, c, : 2 * TRACE] = moved[: 2 * TRACE]
            entry[k + 1, c, 2 * TRACE :] = moved[2 * TRACE :] + old[2 * TRACE :]

    def climbing(k, c):
        left, right = ordered(k, c)
        back = left[:TRACE]
        turned = low(multiply(right[:TRACE, :TRACE], to_low(back)))
        climb[k, c] = turned + high(right[:TRACE]) + keep(lanes((TRACE, WIDE)) >= 2 * TRACE, back)

    def climber(packed_climb):
        return jnp.concatenate([to_low(packed_climb), packed_climb], axis=0)

    alike = lax.div(row_face, FACE) == lax.div(lane_face, FACE)
    small_row = rows((FACE, TRACE))
    small_lane = lax.rem(lanes((FACE, TRACE)), FACE)

    def turn(e):
        chosen = (source_of(orient[e % cells, e // cells], small_row) == small_lane).astype(F32)
        turns[e] = keep(alike, jnp.concatenate([chosen] * VARS, axis=0))

    def remote(source, target, send, recv, device):
        return pltpu.make_async_remote_copy(
            src_ref=source, dst_ref=target, send_sem=send, recv_sem=recv,
            device_id=device, device_id_type=pl.DeviceIdType.MESH,
        )

    sent = []
    pending = {}
    climb_copies = {}

    def dispatch(k, c, part):
        device = (partners[k], column_at)
        if part == 0:
            held_rows, held_lanes = pl.ds(0, ROWS), pl.ds(0, 128)
        elif k < rounds - 1:
            held_rows, held_lanes = pl.ds(0, ROWS), pl.ds(128, 128)
        else:
            held_rows, held_lanes = pl.ds(TRACE, 8), pl.ds(128, 128)
        copy = remote(
            mine.at[k, c, held_rows, held_lanes], theirs.at[k, c, held_rows, held_lanes],
            send_sem.at[k, c, part], recv_sem.at[k, c, part], device,
        )
        copy.start()
        sent.append(copy)
        pending.setdefault((k, c), []).append(copy)

    sides_met = jnp.minimum(column_at, 1) + jnp.minimum(width - 1 - column_at, 1)
    ready(column_of(0), early)
    for c in range(1, cells):
        fetch(column_of(c), early)
    lift_copies[1].start()
    fetch(order, late)
    pick_copy.start()
    throughs = [passing(e) for e in column_of(0)]
    spread_jacobians(0)
    for e, through in zip(column_of(0), throughs):
        ending(e, 0, through)
    for c in range(cells):
        steps = chain(c)
        if c + 1 < cells:
            ready(column_of(c + 1), early)
            spread_jacobians(c + 1)
            throughs = []
            for e in column_of(c + 1):
                next(steps, None)
                throughs.append(passing(e))
            for e, through in zip(column_of(c + 1), throughs):
                next(steps, None)
                ending(e, 0, through)
        for _ in steps:
            pass
        if c == 0:
            pl.semaphore_wait(barrier, met_count + sides_met)
        dispatch(0, c, 1)
        dispatch(0, c, 0)

    lift_copies[1].wait()
    input_copies[2].wait()
    packed[rest_at:] = pack_left(lifts[2:4].reshape(2 * TRACE, BLOCK))
    ready(order, late)
    if rounds == 1:
        for c in range(cells):
            entry[0, c] = jnp.concatenate([eye_low, eye_high, jnp.zeros((8, WIDE), F32)], axis=0)

    answering = [responses(c) for c in range(cells)]

    def stage(index):
        if index < elements:
            rest_pass(order[index])
        if 0 < index <= elements:
            rest_end(order[index - 1])
        if index > 1:
            finish(order[index - 2])
        for steps in answering:
            next(steps, None)

    def finish_answers():
        for steps in answering:
            for _ in steps:
                pass

    def compose(e):
        drop[e] = multiply(sides[e, 0, :, :HALF], zmat[e])

    tasks = []

    def later(cost, function, *values):
        tasks.append((cost, functools.partial(function, *values)))

    for index in range(elements + 2):
        later(0.65, stage, index)
    later(0.05, finish_answers)
    for e in range(elements):
        later(0.03, turn, e)
    for e in range(elements):
        later(0.1, compose, e)

    def work(budget):
        while tasks and (budget is None or tasks[0][0] <= budget):
            cost, task = tasks.pop(0)
            task()
            if budget is not None:
                budget -= cost

    for k in range(rounds):
        for c in range(cells):
            work(None if k == rounds - 1 and c == cells - 1 else 2.0 if k == c == 0 else 0.7)
            for copy in pending[k, c]:
                copy.wait_recv()
            if k < rounds - 1:
                left, right = ordered(k, c)
                first, upper = join(left, right)
                mine[k + 1, c, :, 128:] = upper[:, 128:]
                dispatch(k + 1, c, 1)
                mine[k + 1, c, :, :128] = (upper + join_low(left, first))[:, :128]
                dispatch(k + 1, c, 0)
                firsts[k, c] = first
                level(k, c)
                if k == 0 and c == cells - 1:
                    for other in range(cells):
                        climbing(k, other)
                        copy = remote(
                            climb.at[k, other], climb_got.at[k, other],
                            climb_send.at[k, other], climb_recv.at[k, other], (partners[k + 1], column_at),
                        )
                        copy.start()
                        sent.append(copy)
                        climb_copies[k, other] = copy
    work(None)

    top = rounds - 1
    top_flag = bits[top] == 1

    def meet(z_ours, z_other, flag):
        z_left, z_right = jnp.where(flag, z_other, z_ours), jnp.where(flag, z_ours, z_other)
        return low(z_right) + high(z_left), low(z_left) + high(z_right)

    z_ours = stack([mine[top, c, TRACE : TRACE + 1] for c in range(cells)])
    z_other = stack([theirs[top, c, TRACE : TRACE + 1] for c in range(cells)])
    met, _ = meet(z_ours, z_other, top_flag)
    turned = each(met, [below(low(theirs[top, c, :TRACE])) for c in range(cells)])
    arrived = jnp.where(top_flag, high(met), low(met + turned))
    z_in = each(arrived, [entry[top, c, : 2 * TRACE] for c in range(cells)]) + stack(
        [entry[top, c, 2 * TRACE : 2 * TRACE + 1] for c in range(cells)]
    )
    column = z_in.T
    for layer in range(layers):
        for c in range(cells):
            e = at(layer, c)
            for h in range(2):
                x[h, e : e + 1, :] = (
                    y[h, e : e + 1, :]
                    + full[e, h, 2 * TRACE : 2 * TRACE + 1]
                    + apply(column[: 2 * TRACE, c : c + 1], full[e, h, : 2 * TRACE])
                )

    pick_copy.wait()
    cross = jnp.zeros((elements, WIDE), F32)
    for h in range(2):
        x_high, x_low = split(x[h, :, :HALF])
        cross = cross + (
            jnp.dot(x_high, pick[h], preferred_element_type=F32)
            + jnp.dot(x_low, pick[h], preferred_element_type=F32)
        )
    traces[...] = cross[:, 128:]
    column = cross[:, :128].T
    for e in range(elements):
        backs[e : e + 1, :TRACE] = apply(column[:TRACE, e : e + 1], turns[e])
    up = remote(traces, got_high, cross_sems.at[0], cross_sems.at[1], (place, lax.rem(column_at + 1, width)))
    down = remote(backs, got_back, cross_sems.at[2], cross_sems.at[3], (place, lax.rem(column_at + width - 1, width)))

    @pl.when(column_at < width - 1)
    def _():
        up.start()

    @pl.when(column_at > 0)
    def _():
        down.start()

    def prepare(g):
        for k in groups[g]:
            for c in range(cells):
                reach_level(k, c)
                if 0 < k < top:
                    climbing(k, c)

    prepare(0)
    for layer in range(layers):
        for c in range(cells):
            e = at(layer, c)
            if c > 0:
                from_left[e : e + 1, :] = traces[e - 1 : e, :]
            if c < cells - 1:
                from_right[e : e + 1, :] = backs[e + 1 : e + 2, :]
    firsts_at = [layer * cells for layer in range(layers)]
    lasts_at = [layer * cells + cells - 1 for layer in range(layers)]

    @pl.when(column_at > 0)
    def _():
        up.wait_recv()
        for one, two in zip(firsts_at, lasts_at):
            from_left[one : one + 1, :] = got_high[two : two + 1, :]

    @pl.when(column_at == 0)
    def _():
        for one in firsts_at:
            from_left[one : one + 1, :] = jnp.zeros((1, 128), F32)

    @pl.when(column_at < width - 1)
    def _():
        down.wait_recv()
        for one, two in zip(firsts_at, lasts_at):
            from_right[two : two + 1, :] = got_back[one : one + 1, :]

    @pl.when(column_at == width - 1)
    def _():
        for two in lasts_at:
            from_right[two : two + 1, :] = jnp.zeros((1, 128), F32)

    left_columns = from_left[...].T
    right_columns = from_right[...].T

    def loaded(e, h):
        return y[h, e : e + 1, :] - (
            apply(left_columns[:TRACE, e : e + 1], sides[e, h, :TRACE])
            + apply(right_columns[:TRACE, e : e + 1], sides[e, h, TRACE:])
        )

    def dropped(e):
        return apply(left_columns[:TRACE, e : e + 1], drop[e, :TRACE]) + apply(
            right_columns[:TRACE, e : e + 1], drop[e, TRACE:]
        )

    z_mine[0] = stack([
        mine[0, c, TRACE : TRACE + 1] - functools.reduce(jnp.add, [dropped(at(layer, c)) for layer in range(layers)])
        for c in range(cells)
    ])

    state = {}

    def gathered(layer):
        return stack([y[0, at(layer, c) : at(layer, c) + 1, :] for c in range(cells)])

    def local_sweeps():
        for e in range(elements):
            y[0, e : e + 1, :] = loaded(e, 0)
        forward = [gathered(0)]
        for layer in range(1, layers):
            step = each(forward[-1], [below(ends[at(layer, c), 0, TRACE:]) for c in range(cells)])
            forward.append(step + gathered(layer))
        backward = jnp.zeros((8, WIDE), F32)
        for layer in reversed(range(layers)):
            before = high(forward[layer - 1]) if layer else jnp.zeros((8, WIDE), F32)
            state[layer] = backward + before
            if layer == last:
                backward = low(forward[layer])
            elif layer:
                inverse = [
                    jnp.concatenate([ends[at(layer, c), 0, :TRACE], jnp.zeros((TRACE, WIDE), F32)], axis=0)
                    for c in range(cells)
                ]
                backward = low(each(backward, inverse) + forward[layer])

    def local_rest():
        for e in range(elements):
            y[1, e : e + 1, :] = loaded(e, 1)

    def local_settle():
        local_rest()
        for layer in range(layers):
            column = state[layer].T
            for c in range(cells):
                e = at(layer, c)
                for h in range(2):
                    x[h, e : e + 1, :] = y[h, e : e + 1, :] + apply(column[: 2 * TRACE, c : c + 1], ends[e, h])

    for task in (local_sweeps, local_settle):
        later(0, task)
    z_in = jnp.zeros((8, WIDE), F32)
    for g, group in enumerate(groups):
        copies = [
            remote(z_mine.at[g], z_theirs.at[g, i], z_send.at[g, i], z_recv.at[g, i], (partner, column_at))
            for i, partner in enumerate(friends[g])
        ]
        for copy in copies:
            copy.start()
            sent.append(copy)
        if g + 1 < len(groups):
            prepare(g + 1)
            tasks.pop(0)[1]() if tasks else None
        else:
            work(None)
        k = group[0]
        if len(group) == 2:
            for c in range(cells):
                climb_copies[k, c].wait_recv()
        for copy in copies:
            copy.wait_recv()
        flag = bits[k] == 1
        met, kept = meet(z_mine[g], z_theirs[g, 0], flag)
        z_in = z_in + each(met, [reach[k, c] for c in range(cells)])
        if len(group) == 2:
            both, stays = meet(z_theirs[g, 1], z_theirs[g, 2], flag)
            ours = kept + each(met, [climber(climb[k, c]) for c in range(cells)])
            other = stays + each(both, [climber(climb_got[k, c]) for c in range(cells)])
            k = group[1]
            met, kept = meet(ours, other, bits[k] == 1)
            z_in = z_in + each(met, [reach[k, c] for c in range(cells)])
        if k < top:
            z_mine[g + 1] = kept + each(met, [climber(climb[k, c]) for c in range(cells)])

    column = z_in.T
    for layer in range(layers):
        for c in range(cells):
            e = at(layer, c)
            for h in range(2):
                x[h, e : e + 1, :] = x[h, e : e + 1, :] + apply(
                    column[: 2 * TRACE, c : c + 1], full[e, h, : 2 * TRACE]
                )
    for slot, i in enumerate(SLOTS):
        for v in range(VARS):
            target = (v * EXTENT + i) * FACE
            source = (slot % 2) * TRACE + v * FACE
            natural[:, target : target + FACE] = x[slot // 2, :, source : source + FACE]
    for layer in range(layers):
        out[layer] = natural[layer * cells : (layer + 1) * cells, :]

    for copy in sent:
        copy.wait_send()

    @pl.when(column_at < width - 1)
    def _():
        up.wait_send()

    @pl.when(column_at > 0)
    def _():
        down.wait_send()


def picker():
    table = np.zeros((2, HALF, WIDE), np.float32)
    for slot, i in enumerate(SLOTS):
        for v in range(VARS):
            for k in range(EXTENT):
                source = (slot % 2) * TRACE + v * FACE + k
                target = v * FACE + i * EXTENT + k
                table[slot // 2, source, target] = 1.0
                table[slot // 2, source + (EXTENT - 1) * EXTENT, 128 + target] = 1.0
    return table


def on_device(width, count, vector, inverses, lift_maps, jacobians, orient):
    layers, cells = vector.shape[:2]
    elements = layers * cells
    rounds = count.bit_length() - 1
    inv = inverses.reshape(elements, VARS, EXTENT, FACE, BLOCK)
    flat = jacobians.transpose(0, 1, 3, 4, 2, 5).reshape(elements, VARS, VARS, 4, FACE)
    pick = jnp.asarray(picker(), BF16)
    vec_rows = -(-elements // 16) * 16
    depth = 4 * TRACE + vec_rows
    vmem = pl.BlockSpec(memory_space=pltpu.VMEM)
    hbm = pl.BlockSpec(memory_space=pltpu.HBM)
    tall = 2 * TRACE + 8
    groups = max(1, rounds - 1)
    result = pl.pallas_call(
        functools.partial(kernel, layers, cells, width, rounds),
        out_shape=pltpu.VMEM((layers, cells, BLOCK), F32),
        in_specs=[hbm] * 6,
        out_specs=vmem,
        scratch_shapes=[
            pltpu.VMEM((elements, EXTENT, VARS, FACE, BLOCK), F32),
            pltpu.SemaphoreType.DMA((elements, EXTENT)),
            pltpu.VMEM((4, TRACE, BLOCK), F32),
            pltpu.SemaphoreType.DMA((2,)),
            pltpu.VMEM((2, HALF, WIDE), BF16),
            pltpu.SemaphoreType.DMA((1,)),
            pltpu.VMEM((layers, cells, BLOCK), F32),
            pltpu.VMEM((elements, VARS, VARS, 4, FACE), F32),
            pltpu.SMEM((cells, layers), jnp.int32),
            pltpu.SemaphoreType.DMA((3,)),
            pltpu.VMEM((vec_rows, BLOCK), F32),
            pltpu.VMEM((elements, VARS, 8, WIDE), F32),
            pltpu.VMEM((depth, 4 * WIDE), BF16),
            pltpu.VMEM((elements, HALF, 4 * WIDE), BF16),
            pltpu.VMEM((elements, 2, 2 * TRACE, WIDE), F32),
            pltpu.VMEM((elements, 2, 2 * TRACE, WIDE), F32),
            pltpu.VMEM((elements, tall, WIDE), F32),
            pltpu.VMEM((elements, 2, tall, WIDE), F32),
            pltpu.VMEM((2, elements, WIDE), F32),
            pltpu.VMEM((2, elements, WIDE), F32),
            pltpu.VMEM((rounds, cells, tall, WIDE), F32),
            pltpu.VMEM((rounds, cells, TRACE, WIDE), F32),
            pltpu.VMEM((rounds, cells, TRACE, WIDE), F32),
            pltpu.SemaphoreType.DMA((rounds, cells)),
            pltpu.SemaphoreType.DMA((rounds, cells)),
            pltpu.VMEM((rounds, cells, 2 * TRACE, WIDE), F32),
            pltpu.VMEM((elements, 2 * TRACE, WIDE), F32),
            pltpu.VMEM((elements, 2 * TRACE, WIDE), F32),
            pltpu.VMEM((rounds, cells, ROWS, WIDE), F32),
            pltpu.VMEM((rounds, cells, ROWS, WIDE), F32),
            pltpu.VMEM((rounds, cells, ROWS, WIDE), F32),
            pltpu.SemaphoreType.DMA((rounds, cells, 2)),
            pltpu.SemaphoreType.DMA((rounds, cells, 2)),
            pltpu.VMEM((groups, 8, WIDE), F32),
            pltpu.VMEM((groups, 3, 8, WIDE), F32),
            pltpu.SemaphoreType.DMA((groups, 3)),
            pltpu.SemaphoreType.DMA((groups, 3)),
            pltpu.VMEM((elements, TRACE, TRACE), F32),
            pltpu.VMEM((elements, 128), F32),
            pltpu.VMEM((elements, 128), F32),
            pltpu.VMEM((elements, 128), F32),
            pltpu.VMEM((elements, 128), F32),
            pltpu.VMEM((elements, 128), F32),
            pltpu.VMEM((elements, 128), F32),
            pltpu.SemaphoreType.DMA((4,)),
            pltpu.VMEM((elements, BLOCK), F32),
        ],
        compiler_params=pltpu.CompilerParams(
            collective_id=0, has_side_effects=True, vmem_limit_bytes=62 * 1024 * 1024
        ),
    )(inv, vector, lift_maps.transpose(0, 2, 1), flat, orient.T, pick)
    return result


def solution(mesh):
    in_specs = (
        P("stream", "cross", None),
        P("stream", "cross", None, None),
        P(),
        P("stream", "cross", None, None, None, None),
        P("stream", "cross"),
    )
    out_specs = P("stream", "cross", None)
    return jax.shard_map(
        functools.partial(on_device, mesh.shape["cross"], mesh.shape["stream"]),
        mesh=mesh, in_specs=in_specs, out_specs=out_specs, check_vma=False,
    )
```
